256 devices in a mesh: slab: 4 (over z_lo, core), modes: 64 (over z_hi, y, x).
Axes of the slice: x: 4, y: 4, z: 8 (z_hi: 4, z_lo: 2; z = z_hi * 2 + z_lo), core: 2. Of those that a mesh axis runs over, the one named last changes fastest.
Arguments:
- occupation_prior: float32 [512, 32768], P('slab', 'modes'), may hold values from -6 to 6
- coupling: bfloat16 [256, 64, 128, 128], P('modes'), may hold values from -0.1875 to 0.1875
- pattern: int32 [256, 64], P('modes'), may hold values from 0 to 3
- pseudo_weights: float32 [32768], P('modes'), may hold values from -0.03125 to 0.03125
- equilibrium_slope: float32 [32768], replicated, may hold values from 0.3 to 3
- direction: int32 [256], P('modes'), may hold values from 0 to 1
- stream_rate: float32 [32768], P('modes'), may hold values from 0.15 to 0.95
- inscatter: float32 [256, 128, 128], P('modes'), may hold values from -0.125 to 0.125
- inflow_low: float32 [4, 32768], P(None, 'modes'), may hold values from -6 to 6
- inflow_high: float32 [4, 32768], P(None, 'modes'), may hold values from -6 to 6
- front_of_row: int32 [16], replicated, may hold values from 0 to 3
Outputs:
- swept: float32 [512, 32768], P('slab', 'modes')
The draws below stay inside these ranges and needn't reach their ends.
Inputs may be any that keep to these rules, and one draw needn't show every extreme that they name: `pattern`: each entry names one of the 4 blocks of a group.
All inputs are finite; a program needn't handle non-finite values.
Results may differ from the reference program's by a relative error of at most 0.002.
Values sent between devices are 32-bit elements; how exact they have to be, the bound alone decides.
No kernel may reach another device: no remote copies, remote signals or barrier semaphores. Data moves between devices by JAX's collectives and lax.ppermute only.
A program may use at most 128 MiB of HBM per device.

```python
import math
import jax
import jax.numpy as jnp
from jax import lax

BLK = 128
SHELL = 4
GROUPS = 64
NBLK = 256
MODES = 32768
LAT = 16
LATERAL_FRONTS = 4
NX = 32
CELLS = 512


def plant(values, own_key, smallest, largest):
    dims = values.shape
    spot = [jax.random.randint(jax.random.fold_in(own_key, axis), (), 0, dims[axis]) for axis in range(len(dims))]
    values = values.at[tuple(spot)].set(smallest)
    longest = dims.index(max(dims))
    spot[longest] = (spot[longest] + 1) % dims[longest]
    return values.at[tuple(spot)].set(largest)


def raised(drawn, rng, source, target, blocks, factor):
    owner, partner = [(jnp.arange(drawn.shape[dim]) // (drawn.shape[dim] // blocks)).reshape([-1 if axis == dim else 1 for axis in range(drawn.ndim)]) for dim in (source, target)]
    chosen = jax.random.permutation(rng, blocks)[partner]
    strong = (owner == chosen) | (owner == (partner + blocks // 2) % blocks)
    return jnp.where(strong, factor * drawn, drawn)


def levels(key, dims, split, least, largest):
    level = 1.0
    for position, parts in split:
        draws = jax.random.uniform(jax.random.fold_in(jax.random.fold_in(key, 6), position), (parts,), jnp.float32, least / len(split), largest / len(split))
        level = level * jnp.repeat(jnp.exp(draws), dims[position] // parts).reshape((-1,) + (1,) * (len(dims) - 1 - position))
    return level


def scatter_about(key, extent, width, limit, shards=(), kind=jnp.bfloat16):
    factor_of = levels(key, extent, shards, -0.22, 0.18) if shards else 1.0
    values = jax.random.normal(key, extent, jnp.float32) * width * factor_of
    return jnp.minimum(jnp.maximum(values, -limit), limit).astype(kind)


def gaussian_with(key, extent, deviation, bound, pieces, heavy, kind=jnp.bfloat16):
    drawn = deviation * jax.random.normal(key, extent, jnp.float32)
    if pieces:
        drawn = drawn * levels(key, extent, pieces, -0.22, 0.18)
    return jnp.clip(raised(drawn, jax.random.fold_in(key, 3), *heavy), -bound, bound).astype(kind)


def setup_inputs(seed: int = 0) -> dict:
    key_of = jax.random.split(jax.random.key(seed), 12)
    occupation_prior = scatter_about(key_of[0], (CELLS, MODES), 1.0, 6.0, ((0, 4), (1, 64)), jnp.float32)
    coupling = gaussian_with(key_of[1], (NBLK, GROUPS, BLK, BLK), (BLK * GROUPS) ** -0.5, 0.1875, ((0, 64),), (0, 1, 64, 4.0))
    pattern = plant(jax.random.randint(key_of[2], (NBLK, GROUPS), 0, SHELL), jax.random.fold_in(key_of[2], 1), 0, SHELL - 1).astype(jnp.int32)
    pseudo_weights = scatter_about(key_of[3], (MODES,), MODES ** -0.5, 0.03125, ((0, 64),), jnp.float32)
    equilibrium_slope = jnp.clip(jnp.exp(jax.random.uniform(key_of[4], (MODES,), jnp.float32, math.log(0.3), math.log(3.0))), 0.3, 3.0)
    direction = plant(jax.random.randint(key_of[5], (NBLK,), 0, 2), jax.random.fold_in(key_of[5], 1), 0, 1).astype(jnp.int32)
    stream_rate = jnp.clip(0.15 + 0.79999998 * jax.random.uniform(key_of[6], (MODES,), jnp.float32) ** levels(key_of[6], (MODES,), ((0, 64),), -0.2, 0.2), 0.15, 0.95)
    inscatter = scatter_about(key_of[7], (NBLK, BLK, BLK), (16 * BLK) ** -0.5, 0.125, ((0, 64),), jnp.float32)
    inflow_low = scatter_about(key_of[8], (LATERAL_FRONTS, MODES), 1.0, 6.0, ((1, 64),), jnp.float32)
    inflow_high = scatter_about(key_of[9], (LATERAL_FRONTS, MODES), 1.0, 6.0, ((1, 64),), jnp.float32)
    front_of_row = plant(jax.random.randint(key_of[10], (LAT,), 0, LATERAL_FRONTS), jax.random.fold_in(key_of[10], 1), 0, LATERAL_FRONTS - 1).astype(jnp.int32)
    return dict(occupation_prior=occupation_prior, coupling=coupling, pattern=pattern, pseudo_weights=pseudo_weights, equilibrium_slope=equilibrium_slope, direction=direction, stream_rate=stream_rate, inscatter=inscatter, inflow_low=inflow_low, inflow_high=inflow_high, front_of_row=front_of_row)


def reference(occupation_prior, coupling, pattern, pseudo_weights, equilibrium_slope, direction, stream_rate, inscatter, inflow_low, inflow_high, front_of_row):
    cell_count = occupation_prior.shape[0]
    rounded = lax.optimization_barrier(occupation_prior.astype(jnp.bfloat16)).astype(jnp.float32)
    group_index = jnp.arange(GROUPS, dtype=jnp.int32)

    def add_block(totals, block_index):
        source_rows = lax.dynamic_slice_in_dim(rounded, (block_index * BLK).astype(jnp.int32), BLK, 1)
        weights = coupling[block_index].astype(jnp.float32)
        product = jnp.einsum('ck,gkl->cgl', source_rows, weights, precision=lax.Precision.HIGHEST)
        totals = totals.at[:, group_index, pattern[block_index]].add(product)
        return totals, None

    totals, _ = lax.scan(add_block, jnp.zeros((cell_count, GROUPS, SHELL, BLK), jnp.float32), jnp.arange(NBLK, dtype=jnp.int32))
    collided_branches = totals.reshape(cell_count, MODES)
    branch_pseudo_warmth = jnp.sum(occupation_prior * pseudo_weights[None, :], axis=1)
    gain_contribution = collided_branches + branch_pseudo_warmth[:, None] * equilibrium_slope[None, :]
    source_cells = gain_contribution.reshape(NX, LAT, NBLK, BLK)
    forward_mask = (direction == 1)[None, None, :, None]
    ordered = jnp.where(forward_mask, source_cells, source_cells[::-1])
    row_picks = (front_of_row[:, None] == jnp.arange(LATERAL_FRONTS, dtype=jnp.int32)[None, :]).astype(jnp.float32)
    wall_low = jnp.dot(row_picks, inflow_low, precision=lax.Precision.HIGHEST).reshape(LAT, NBLK, BLK)
    wall_high = jnp.dot(row_picks, inflow_high, precision=lax.Precision.HIGHEST).reshape(LAT, NBLK, BLK)
    face_start = jnp.where(forward_mask[0], wall_low, wall_high)
    rate_table = stream_rate.reshape(NBLK, BLK)
    transfer = jnp.eye(BLK, dtype=jnp.float32)[None] + inscatter

    def sweep_step(face_now, layer_source):
        face_next = jnp.einsum('ybk,bkl->ybl', layer_source + rate_table * face_now, transfer, precision=lax.Precision.HIGHEST)
        return face_next, face_next

    _, stacked = lax.scan(sweep_step, face_start, ordered)
    result = jnp.where(forward_mask, stacked, stacked[::-1])
    return result.reshape(cell_count, MODES)
```

```python
import functools

import jax
import jax.numpy as jnp
from jax import lax
from jax.experimental import pallas as pl
from jax.experimental.pallas import tpu as pltpu
from jax.sharding import PartitionSpec as P

BLK = 128
SHELL = 4
ZN = 4
PLANE = 16
PER_STEP = 4
LAYERS = 8
LATERAL = 16
WIDTH = SHELL * BLK
CELL = LAYERS * LATERAL
HIGH = lax.Precision.HIGHEST
PLANES = [[z * PLANE + i for i in range(PLANE)] for z in range(ZN)]


def z_route(step):
    return [
        (z * PLANE + i, ((z + step) % ZN) * PLANE + i) for z in range(ZN) for i in range(PLANE)
    ]


def partial_kernel(steps_ref, pattern_ref, x_ref, weight_ref, slope_ref, coupling_ref, out_ref, rounded, warmth):
    step = pl.program_id(0)

    @pl.when(step == 0)
    def _():
        prior = x_ref[...]
        rounded[...] = prior.astype(jnp.bfloat16)
        total = jnp.sum(prior * weight_ref[...], axis=1, keepdims=True)
        warmth[...] = jnp.broadcast_to(total, warmth.shape)

    first = steps_ref[step] * PER_STEP
    heat = warmth[...]
    for g in range(PER_STEP):
        for t in range(SHELL):
            lanes = pl.ds(t * BLK, BLK)
            out_ref[0, g, :, lanes] = heat * slope_ref[pl.ds(g, 1), lanes]
        for b in range(SHELL):
            product = jnp.dot(
                rounded[:, pl.ds(b * BLK, BLK)],
                coupling_ref[b, g],
                preferred_element_type=jnp.float32,
            )
            where = pattern_ref[b, first + g]
            lanes = pl.ds(pl.multiple_of(where * BLK, BLK), BLK)
            out_ref[0, g, :, lanes] += product


def partial_sums(z, distances, pattern, prior, weights, slope, coupling):
    per_plane = PLANE // PER_STEP
    count = len(distances)
    steps = jnp.concatenate(
        [((z + d) % ZN) * per_plane + jnp.arange(per_plane, dtype=jnp.int32) for d in distances]
    )
    out = pl.pallas_call(
        partial_kernel,
        grid_spec=pltpu.PrefetchScalarGridSpec(
            num_scalar_prefetch=2,
            grid=(count * per_plane,),
            in_specs=[
                pl.BlockSpec((CELL, WIDTH), lambda i, s, p: (0, 0)),
                pl.BlockSpec((1, WIDTH), lambda i, s, p: (0, 0)),
                pl.BlockSpec((None, PER_STEP, WIDTH), lambda i, s, p: (s[i], 0, 0)),
                pl.BlockSpec((SHELL, PER_STEP, BLK, BLK), lambda i, s, p: (0, s[i], 0, 0)),
            ],
            out_specs=pl.BlockSpec(
                (1, PER_STEP, CELL, WIDTH), lambda i, s, p: (i // per_plane, i % per_plane, 0, 0)
            ),
            scratch_shapes=[
                pltpu.VMEM((CELL, WIDTH), jnp.bfloat16),
                pltpu.VMEM((CELL, BLK), jnp.float32),
            ],
        ),
        out_shape=jax.ShapeDtypeStruct((count, PLANE, CELL, WIDTH), jnp.float32),
        cost_estimate=pl.CostEstimate(
            flops=2 * CELL * WIDTH * BLK * PLANE * count,
            bytes_accessed=count * PLANE * CELL * WIDTH * 4,
            transcendentals=0,
        ),
        name="partial_sums",
    )(steps, pattern, prior, weights, slope, coupling)
    return out


def powers_kernel(rate_ref, inscatter_ref, out_ref):
    row = lax.broadcasted_iota(jnp.int32, (BLK, BLK), 0)
    column = lax.broadcasted_iota(jnp.int32, (BLK, BLK), 1)
    unit = jnp.where(row == column, 1.0, 0.0).astype(jnp.float32)
    transfer = [unit + inscatter_ref[b] for b in range(SHELL)]
    now = list(transfer)
    for k in range(LAYERS):
        for b in range(SHELL):
            out_ref[b, k] = now[b]
            if k + 1 < LAYERS:
                now[b] = jnp.dot(
                    now[b] * rate_ref[:, pl.ds(b * BLK, BLK)],
                    transfer[b],
                    precision=HIGH,
                    preferred_element_type=jnp.float32,
                )


def last_kernel(direction_ref, source_ref, power_ref, out_ref):
    for b in range(SHELL):
        lanes = pl.ds(b * BLK, BLK)
        up = direction_ref[b] == 1
        total = jnp.zeros((LATERAL, BLK), jnp.float32)
        for t in range(LAYERS):
            k = jnp.where(up, LAYERS - 1 - t, t)
            total += jnp.dot(
                source_ref[pl.ds(t * LATERAL, LATERAL), lanes],
                power_ref[b, k],
                precision=HIGH,
                preferred_element_type=jnp.float32,
            )
        out_ref[:, lanes] = total


def particular_kernel(direction_ref, source_ref, rate_ref, power_ref, out_ref):
    now = [jnp.zeros((LATERAL, BLK), jnp.float32) for _ in range(SHELL)]
    for t in range(LAYERS):
        for b in range(SHELL):
            lanes = pl.ds(b * BLK, BLK)
            at = jnp.where(direction_ref[b] == 1, t, LAYERS - 1 - t)
            rows = pl.ds(pl.multiple_of(at * LATERAL, LATERAL), LATERAL)
            now[b] = jnp.dot(
                source_ref[rows, lanes] + rate_ref[:, lanes] * now[b],
                power_ref[b, 0],
                precision=HIGH,
                preferred_element_type=jnp.float32,
            )
            out_ref[rows, lanes] = now[b]


def finish_kernel(
    direction_ref, slab_ref, wall_ref, one_ref, two_ref, three_ref, rate_ref, particular_ref, power_ref, out_ref, faces
):
    for k, face in enumerate((one_ref, two_ref, three_ref)):
        faces[k] = face[...]
    slab = slab_ref[0]
    now = [wall_ref[:, pl.ds(b * BLK, BLK)] for b in range(SHELL)]
    for n in range(3):
        for b in range(SHELL):
            lanes = pl.ds(b * BLK, BLK)
            up = direction_ref[b] == 1
            k = jnp.where(up, 2 - n, n)
            active = jnp.where(up, (k + 1 <= slab).astype(jnp.int32), (k + 1 > slab).astype(jnp.int32))
            moved = faces[k, :, lanes] + jnp.dot(
                now[b] * rate_ref[:, lanes],
                power_ref[b, LAYERS - 1],
                precision=HIGH,
                preferred_element_type=jnp.float32,
            )
            now[b] = jnp.where(active == 1, moved, now[b])
    for b in range(SHELL):
        lanes = pl.ds(b * BLK, BLK)
        up = direction_ref[b] == 1
        scaled = now[b] * rate_ref[:, lanes]
        for t in range(LAYERS):
            k = jnp.where(up, t, LAYERS - 1 - t)
            rows = pl.ds(t * LATERAL, LATERAL)
            out_ref[rows, lanes] = particular_ref[rows, lanes] + jnp.dot(
                scaled, power_ref[b, k], precision=HIGH, preferred_element_type=jnp.float32
            )


SMEM = pl.BlockSpec(memory_space=pltpu.SMEM)
VMEM = pl.BlockSpec(memory_space=pltpu.VMEM)


def small_call(kernel, out_shape, specs, scratch=(), flops=0, name=None):
    return pl.pallas_call(
        kernel,
        in_specs=specs,
        out_specs=VMEM,
        out_shape=jax.ShapeDtypeStruct(out_shape, jnp.float32),
        scratch_shapes=list(scratch),
        cost_estimate=pl.CostEstimate(flops=flops, bytes_accessed=3 << 20, transcendentals=0),
        name=name,
    )


def per_device(
    occupation_prior,
    coupling,
    pattern,
    pseudo_weights,
    equilibrium_slope,
    direction,
    stream_rate,
    inscatter,
    inflow_low,
    inflow_high,
    front_of_row,
):
    modes = lax.axis_index("modes")
    slab = lax.axis_index("slab").astype(jnp.int32)
    z = (modes // PLANE).astype(jnp.int32)
    weights = pseudo_weights.reshape(1, WIDTH)
    rate = stream_rate.reshape(1, WIDTH)
    slope = equilibrium_slope.reshape(ZN * PLANE // PER_STEP, PER_STEP, WIDTH)
    make = functools.partial(
        partial_sums,
        pattern=pattern,
        prior=occupation_prior,
        weights=weights,
        slope=slope,
        coupling=coupling,
    )

    def reduced(distances):
        sums = make(z, distances)
        count = len(distances)
        if count > 1:
            sums = sums.swapaxes(0, 1)
        got = lax.psum_scatter(
            sums.reshape(PLANE * count * CELL, WIDTH),
            "modes",
            scatter_dimension=0,
            axis_index_groups=PLANES,
            tiled=True,
        )
        return [got[i * CELL : (i + 1) * CELL] for i in range(count)]

    (far,) = reduced((2,))
    (above,) = reduced((1,))
    (below,) = reduced((3,))
    (mine,) = reduced((0,))
    half = CELL // 2
    far_up = lax.ppermute(far[:half], "modes", z_route(1))
    far_down = lax.ppermute(far[half:], "modes", z_route(-1))
    above = jnp.concatenate([above[:half] + far_up, above[half:]], axis=0)
    below = jnp.concatenate([below[:half], below[half:] + far_down], axis=0)
    from_below = lax.ppermute(above, "modes", z_route(1))
    from_above = lax.ppermute(below, "modes", z_route(-1))
    source = mine + from_below + from_above

    powers = small_call(
        powers_kernel, (SHELL, LAYERS, BLK, BLK), [VMEM, VMEM], flops=200_000_000, name="powers"
    )(rate, inscatter)
    picks = front_of_row[:, None] == jnp.arange(inflow_low.shape[0], dtype=jnp.int32)[None, :]
    ahead = (jnp.repeat(direction, BLK) == 1)[None, :]
    inflow = jnp.where(ahead, inflow_low, inflow_high)
    wall = jnp.sum(jnp.where(picks[:, :, None], inflow[None, :, :], 0.0), axis=1)

    last = small_call(
        last_kernel, (LATERAL, WIDTH), [SMEM, VMEM, VMEM], flops=40_000_000, name="last_face"
    )(direction, source, powers)
    faces = [
        lax.ppermute(last, "slab", [(i, (i + k) % 4) for i in range(4)]) for k in (1, 2, 3)
    ]
    particular = small_call(
        particular_kernel, (CELL, WIDTH), [SMEM, VMEM, VMEM, VMEM], flops=40_000_000, name="particular"
    )(direction, source, rate, powers)
    return small_call(
        finish_kernel,
        (CELL, WIDTH),
        [SMEM, SMEM] + [VMEM] * 7,
        scratch=[pltpu.VMEM((3, LATERAL, WIDTH), jnp.float32)],
        flops=60_000_000,
        name="finish",
    )(direction, slab.reshape(1), wall, *faces, rate, particular, powers)


def solution(mesh):
    placed = (
        P("slab", "modes"),
        P("modes", None, None, None),
        P("modes", None),
        P("modes"),
        P(),
        P("modes"),
        P("modes"),
        P("modes", None, None),
        P(None, "modes"),
        P(None, "modes"),
        P(),
    )
    return jax.shard_map(
        per_device, mesh=mesh, in_specs=placed, out_specs=P("slab", "modes"), check_vma=False
    )
```

```python
import functools

import jax
import jax.numpy as jnp
from jax import lax
from jax.experimental import pallas as pl
from jax.experimental.pallas import tpu as pltpu
from jax.sharding import PartitionSpec as P

BLK = 128
SHELL = 4
SIDE = 4
LAYERS = 8
LATERAL = 16
WIDTH = SHELL * BLK
CELL = LAYERS * LATERAL
HALF = CELL // 2
JOBS = 4
HIGH = lax.Precision.HIGHEST


def route(axis, step):
    pairs = []
    for z in range(SIDE):
        for y in range(SIDE):
            for x in range(SIDE):
                there = [z, y, x]
                there[axis] = (there[axis] + step) % SIDE
                pairs.append(
                    ((z * SIDE + y) * SIDE + x, (there[0] * SIDE + there[1]) * SIDE + there[2])
                )
    return pairs


def send(block, axis, step):
    return lax.ppermute(block, "modes", route(axis, step))


def partial_kernel(addends, groups_ref, pattern_ref, x_ref, weight_ref, *refs):
    slopes, couplings = refs[:JOBS], refs[JOBS : 2 * JOBS]
    added = refs[2 * JOBS : 2 * JOBS + addends]
    outs = refs[2 * JOBS + addends : 3 * JOBS + addends]
    rounded, warmth = refs[3 * JOBS + addends :]
    step = pl.program_id(0)

    @pl.when(step == 0)
    def _():
        prior = x_ref[...]
        rounded[...] = prior.astype(jnp.bfloat16)
        total = jnp.sum(prior * weight_ref[...], axis=1, keepdims=True)
        warmth[...] = jnp.broadcast_to(total, warmth.shape)

    heat = warmth[...]
    for job in range(JOBS):
        group = groups_ref[job, step]
        out_ref = outs[job]
        for t in range(SHELL):
            lanes = pl.ds(t * BLK, BLK)
            start = heat * slopes[job][0, :, lanes]
            if addends:
                start += added[job][0, :, lanes]
            out_ref[0, :, lanes] = start
        for b in range(SHELL):
            product = jnp.dot(
                rounded[:, pl.ds(b * BLK, BLK)],
                couplings[job][b, 0],
                preferred_element_type=jnp.float32,
            )
            where = pattern_ref[b, group]
            lanes = pl.ds(pl.multiple_of(where * BLK, BLK), BLK)
            out_ref[0, :, lanes] += product


def partial_sums(groups, addends, pattern, prior, weights, slope, coupling):
    slope_specs = [
        pl.BlockSpec((1, 1, WIDTH), functools.partial(lambda j, i, g, p: (g[j, i], 0, 0), j))
        for j in range(JOBS)
    ]
    coupling_specs = [
        pl.BlockSpec(
            (SHELL, 1, BLK, BLK), functools.partial(lambda j, i, g, p: (0, g[j, i], 0, 0), j)
        )
        for j in range(JOBS)
    ]
    unit = pl.BlockSpec((1, CELL, WIDTH), lambda i, g, p: (i, 0, 0))
    return pl.pallas_call(
        functools.partial(partial_kernel, len(addends)),
        grid_spec=pltpu.PrefetchScalarGridSpec(
            num_scalar_prefetch=2,
            grid=(SIDE,),
            in_specs=[
                pl.BlockSpec((CELL, WIDTH), lambda i, g, p: (0, 0)),
                pl.BlockSpec((1, WIDTH), lambda i, g, p: (0, 0)),
            ]
            + slope_specs
            + coupling_specs
            + [unit] * len(addends),
            out_specs=[unit] * JOBS,
            scratch_shapes=[
                pltpu.VMEM((CELL, WIDTH), jnp.bfloat16),
                pltpu.VMEM((CELL, BLK), jnp.float32),
            ],
        ),
        out_shape=[jax.ShapeDtypeStruct((SIDE, CELL, WIDTH), jnp.float32)] * JOBS,
        cost_estimate=pl.CostEstimate(
            flops=2 * CELL * WIDTH * BLK * SIDE * JOBS,
            bytes_accessed=SIDE * JOBS * CELL * WIDTH * 6,
            transcendentals=0,
        ),
        name="partial_sums",
    )(groups, pattern, prior, weights, *([slope] * JOBS), *([coupling] * JOBS), *addends)


def powers_kernel(rate_ref, inscatter_ref, out_ref):
    row = lax.broadcasted_iota(jnp.int32, (BLK, BLK), 0)
    column = lax.broadcasted_iota(jnp.int32, (BLK, BLK), 1)
    unit = jnp.where(row == column, 1.0, 0.0).astype(jnp.float32)
    transfer = [unit + inscatter_ref[b] for b in range(SHELL)]
    now = list(transfer)
    for k in range(LAYERS):
        for b in range(SHELL):
            out_ref[b, k] = now[b]
            if k + 1 < LAYERS:
                now[b] = jnp.dot(
                    now[b] * rate_ref[:, pl.ds(b * BLK, BLK)],
                    transfer[b],
                    precision=HIGH,
                    preferred_element_type=jnp.float32,
                )


def last_kernel(direction_ref, source_ref, power_ref, out_ref):
    for b in range(SHELL):
        lanes = pl.ds(b * BLK, BLK)
        up = direction_ref[b] == 1
        total = jnp.zeros((LATERAL, BLK), jnp.float32)
        for t in range(LAYERS):
            k = jnp.where(up, LAYERS - 1 - t, t)
            total += jnp.dot(
                source_ref[pl.ds(t * LATERAL, LATERAL), lanes],
                power_ref[b, k],
                precision=HIGH,
                preferred_element_type=jnp.float32,
            )
        out_ref[:, lanes] = total


def particular_kernel(direction_ref, source_ref, rate_ref, power_ref, out_ref):
    now = [jnp.zeros((LATERAL, BLK), jnp.float32) for _ in range(SHELL)]
    for t in range(LAYERS):
        for b in range(SHELL):
            lanes = pl.ds(b * BLK, BLK)
            at = jnp.where(direction_ref[b] == 1, t, LAYERS - 1 - t)
            rows = pl.ds(pl.multiple_of(at * LATERAL, LATERAL), LATERAL)
            now[b] = jnp.dot(
                source_ref[rows, lanes] + rate_ref[:, lanes] * now[b],
                power_ref[b, 0],
                precision=HIGH,
                preferred_element_type=jnp.float32,
            )
            out_ref[rows, lanes] = now[b]


def finish_kernel(
    direction_ref, slab_ref, wall_ref, one_ref, two_ref, three_ref, rate_ref, particular_ref, power_ref, out_ref, faces
):
    for k, face in enumerate((one_ref, two_ref, three_ref)):
        faces[k] = face[...]
    slab = slab_ref[0]
    now = [wall_ref[:, pl.ds(b * BLK, BLK)] for b in range(SHELL)]
    for n in range(3):
        for b in range(SHELL):
            lanes = pl.ds(b * BLK, BLK)
            up = direction_ref[b] == 1
            k = jnp.where(up, 2 - n, n)
            active = jnp.where(up, (k + 1 <= slab).astype(jnp.int32), (k + 1 > slab).astype(jnp.int32))
            moved = faces[k, :, lanes] + jnp.dot(
                now[b] * rate_ref[:, lanes],
                power_ref[b, LAYERS - 1],
                precision=HIGH,
                preferred_element_type=jnp.float32,
            )
            now[b] = jnp.where(active == 1, moved, now[b])
    for b in range(SHELL):
        lanes = pl.ds(b * BLK, BLK)
        up = direction_ref[b] == 1
        scaled = now[b] * rate_ref[:, lanes]
        for t in range(LAYERS):
            k = jnp.where(up, t, LAYERS - 1 - t)
            rows = pl.ds(t * LATERAL, LATERAL)
            out_ref[rows, lanes] = particular_ref[rows, lanes] + jnp.dot(
                scaled, power_ref[b, k], precision=HIGH, preferred_element_type=jnp.float32
            )


SMEM = pl.BlockSpec(memory_space=pltpu.SMEM)
VMEM = pl.BlockSpec(memory_space=pltpu.VMEM)


def small_call(kernel, out_shape, specs, scratch=(), flops=0, name=None):
    return pl.pallas_call(
        kernel,
        in_specs=specs,
        out_specs=VMEM,
        out_shape=jax.ShapeDtypeStruct(out_shape, jnp.float32),
        scratch_shapes=list(scratch),
        cost_estimate=pl.CostEstimate(flops=flops, bytes_accessed=3 << 20, transcendentals=0),
        name=name,
    )


def per_device(
    occupation_prior,
    coupling,
    pattern,
    pseudo_weights,
    equilibrium_slope,
    direction,
    stream_rate,
    inscatter,
    inflow_low,
    inflow_high,
    front_of_row,
):
    modes = lax.axis_index("modes").astype(jnp.int32)
    slab = lax.axis_index("slab").astype(jnp.int32)
    here = (modes // (SIDE * SIDE), modes // SIDE % SIDE, modes % SIDE)
    weights = pseudo_weights.reshape(1, WIDTH)
    rate = stream_rate.reshape(1, WIDTH)
    slope = equilibrium_slope.reshape(SIDE**3, 1, WIDTH)
    along = jnp.arange(SIDE, dtype=jnp.int32)

    def groups_of(z_step, y_step, x_step):
        z = (here[0] + z_step) % SIDE
        y = (here[1] + y_step) % SIDE
        x = (here[2] + x_step) % SIDE
        return (z * SIDE + y) * SIDE + x

    def make(steps, *addends):
        groups = jnp.stack(
            [
                groups_of(1, along, steps[0]),
                groups_of(2, along, steps[1]),
                groups_of(3, steps[0], along),
                groups_of(0, steps[1], along),
            ]
        )
        return partial_sums(
            groups, addends, pattern, occupation_prior, weights, slope, coupling
        )

    firsts = (2, 2, 1, 1)
    axes = firsts
    far = make((2, 2))
    far_got = [send(far[0], 2, 1), send(far[1], 2, -1), send(far[2], 1, 1), send(far[3], 1, -1)]
    direct = make((3, 1))
    early = [send(direct[0], 2, -1), send(direct[1], 2, 1), send(direct[2], 1, -1), send(direct[3], 1, 1)]
    joined = make((1, 3), *far_got)
    late = [send(joined[0], 2, 1), send(joined[1], 2, -1), send(joined[2], 1, 1), send(joined[3], 1, -1)]
    kept = make((0, 0), *early)

    def second(p, q, p_late, q_late, axis):
        far_p = send(p[2] + p_late[2], axis, 1)
        far_q = send(q[2] + q_late[2], axis, -1)
        near_q = send(q[1] + q_late[1], axis, 1)
        near_p = send(p[3] + p_late[3], axis, -1)
        last_p = send(p[1] + p_late[1] + far_p, axis, 1)
        last_q = send(q[3] + q_late[3] + far_q, axis, -1)
        return (
            p[0] + p_late[0] + near_p + last_p,
            q[0] + q_late[0] + near_q + last_q,
        )

    above, far = second(kept[0], kept[1], late[0], late[1], 1)
    below, mine = second(kept[2], kept[3], late[2], late[3], 2)
    far_up = send(far[:HALF], 0, 1)
    far_down = send(far[HALF:], 0, -1)
    free_up = send(above[HALF:], 0, 1)
    free_down = send(below[:HALF], 0, -1)
    last_up = send(above[:HALF] + far_up, 0, 1)
    last_down = send(below[HALF:] + far_down, 0, -1)
    source = mine + jnp.concatenate([free_down + last_up, free_up + last_down], axis=0)

    powers = small_call(
        powers_kernel, (SHELL, LAYERS, BLK, BLK), [VMEM, VMEM], flops=200_000_000, name="powers"
    )(rate, inscatter)
    picks = front_of_row[:, None] == jnp.arange(inflow_low.shape[0], dtype=jnp.int32)[None, :]
    ahead = (jnp.repeat(direction, BLK) == 1)[None, :]
    inflow = jnp.where(ahead, inflow_low, inflow_high)
    wall = jnp.sum(jnp.where(picks[:, :, None], inflow[None, :, :], 0.0), axis=1)

    last = small_call(
        last_kernel, (LATERAL, WIDTH), [SMEM, VMEM, VMEM], flops=40_000_000, name="last_face"
    )(direction, source, powers)
    faces = [
        lax.ppermute(last, "slab", [(i, (i + k) % 4) for i in range(4)]) for k in (1, 2, 3)
    ]
    particular = small_call(
        particular_kernel, (CELL, WIDTH), [SMEM, VMEM, VMEM, VMEM], flops=40_000_000, name="particular"
    )(direction, source, rate, powers)
    return small_call(
        finish_kernel,
        (CELL, WIDTH),
        [SMEM, SMEM] + [VMEM] * 7,
        scratch=[pltpu.VMEM((3, LATERAL, WIDTH), jnp.float32)],
        flops=60_000_000,
        name="finish",
    )(direction, slab.reshape(1), wall, *faces, rate, particular, powers)


def solution(mesh):
    placed = (
        P("slab", "modes"),
        P("modes", None, None, None),
        P("modes", None),
        P("modes"),
        P(),
        P("modes"),
        P("modes"),
        P("modes", None, None),
        P(None, "modes"),
        P(None, "modes"),
        P(),
    )
    return jax.shard_map(
        per_device, mesh=mesh, in_specs=placed, out_specs=P("slab", "modes"), check_vma=False
    )
```

```python
import functools

import jax
import jax.numpy as jnp
import numpy as np
from jax import lax
from jax.experimental import pallas as pl
from jax.experimental.pallas import tpu as pltpu
from jax.sharding import PartitionSpec as P

BLK = 128
SHELL = 4
SIDE = 4
LAYERS = 8
LATERAL = 16
WIDTH = SHELL * BLK
CELL = LAYERS * LATERAL
HALF = CELL // 2


UPPER = ((0, CELL, 1), (0, HALF, 2))
LOWER = ((0, CELL, 3), (HALF, HALF, 2))


def offsets():
    rows = []
    for steps in ((2, 2), (3, 1), (1, 3), (0, 0)):
        for job in (UPPER, LOWER):
            for pair, step in ((0, steps[0]), (2, steps[1])):
                for _, _, d in job:
                    units = [(d, pair + i % 2, step) for i in range(SIDE)]
                    rows.append(units if job is UPPER else [(z, x, y) for z, y, x in units])
    rows += [[(0, i, step) for i in range(SIDE)] for step in range(SIDE)]
    rows += [[(0, step, i) for i in range(SIDE)] for step in range(SIDE)]
    return np.array(rows, np.int32)


def group_table(here):
    moved = [(place + offsets()[..., axis]) & (SIDE - 1) for axis, place in enumerate(here)]
    return (moved[0] * SIDE + moved[1]) * SIDE + moved[2]


def route(axis, step):
    pairs = []
    for z in range(SIDE):
        for y in range(SIDE):
            for x in range(SIDE):
                there = [z, y, x]
                there[axis] = (there[axis] + step) % SIDE
                pairs.append(
                    ((z * SIDE + y) * SIDE + x, (there[0] * SIDE + there[1]) * SIDE + there[2])
                )
    return pairs


def send(block, axis, step):
    return lax.ppermute(block, "modes", route(axis, step))


def partial_kernel(jobs, first, addends, groups_ref, pattern_ref, x_ref, weight_ref, *refs):
    segments = sum(len(job) for job in jobs)
    slopes, couplings = refs[:segments], refs[segments : 2 * segments]
    refs = refs[2 * segments :]
    added, outs = refs[:addends], refs[addends : addends + len(jobs)]
    rounded, warmth = refs[addends + len(jobs) :]
    step = pl.program_id(0)

    @pl.when(step == 0)
    def _():
        prior = x_ref[...]
        rounded[...] = prior.astype(jnp.bfloat16)
        total = jnp.sum(prior * weight_ref[...], axis=1, keepdims=True)
        warmth[...] = jnp.broadcast_to(total, warmth.shape)

    n = 0
    for index, job in enumerate(jobs):
        out_ref = outs[index]
        base = 0
        for from_row, count, _ in job:
            cells = pl.ds(from_row, count)
            rows = pl.ds(base, count)
            group = groups_ref[first + n, step]
            heat = warmth[cells, :]
            for t in range(SHELL):
                lanes = pl.ds(t * BLK, BLK)
                start = heat * slopes[n][0, :, lanes]
                if addends:
                    start += added[index][0, rows, lanes]
                out_ref[0, rows, lanes] = start
            for b in range(SHELL):
                product = jnp.dot(
                    rounded[cells, pl.ds(b * BLK, BLK)],
                    couplings[n][b, 0],
                    preferred_element_type=jnp.float32,
                )
                where = pattern_ref[b, group]
                lanes = pl.ds(pl.multiple_of(where * BLK, BLK), BLK)
                out_ref[0, rows, lanes] += product
            base += count
            n += 1


def partial_sums(jobs, first, units, addends, groups, pattern, prior, weights, slope, coupling):
    segments = sum(len(job) for job in jobs)
    slope_specs = [
        pl.BlockSpec((1, 1, WIDTH), functools.partial(lambda n, i, g, p: (g[n, i], 0, 0), first + n))
        for n in range(segments)
    ]
    coupling_specs = [
        pl.BlockSpec(
            (SHELL, 1, BLK, BLK), functools.partial(lambda n, i, g, p: (0, g[n, i], 0, 0), first + n)
        )
        for n in range(segments)
    ]
    heights = [sum(count for _, count, _ in job) for job in jobs]
    blocks = [pl.BlockSpec((1, rows, WIDTH), lambda i, g, p: (i, 0, 0)) for rows in heights]
    return pl.pallas_call(
        functools.partial(partial_kernel, jobs, first, len(addends)),
        grid_spec=pltpu.PrefetchScalarGridSpec(
            num_scalar_prefetch=2,
            grid=(units,),
            in_specs=[
                pl.BlockSpec((CELL, WIDTH), lambda i, g, p: (0, 0)),
                pl.BlockSpec((1, WIDTH), lambda i, g, p: (0, 0)),
            ]
            + slope_specs
            + coupling_specs
            + blocks[: len(addends)],
            out_specs=blocks,
            scratch_shapes=[
                pltpu.VMEM((CELL, WIDTH), jnp.bfloat16),
                pltpu.VMEM((CELL, BLK), jnp.float32),
            ],
        ),
        out_shape=[jax.ShapeDtypeStruct((units, rows, WIDTH), jnp.float32) for rows in heights],
        cost_estimate=pl.CostEstimate(
            flops=2 * sum(heights) * units * WIDTH * BLK,
            bytes_accessed=sum(heights) * units * WIDTH * 6,
            transcendentals=0,
        ),
        name="partial_sums",
    )(
        groups,
        pattern,
        prior,
        weights,
        *([slope] * segments),
        *([coupling] * segments),
        *addends,
    )


def powers_kernel(rate_ref, inscatter_ref, high_ref, low_ref):
    row = lax.broadcasted_iota(jnp.int32, (BLK, BLK), 0)
    column = lax.broadcasted_iota(jnp.int32, (BLK, BLK), 1)
    unit = jnp.where(row == column, 1.0, 0.0).astype(jnp.float32)
    now = [unit + inscatter_ref[b] for b in range(SHELL)]
    for k in range(LAYERS):
        for b in range(SHELL):
            high = now[b].astype(jnp.bfloat16)
            high_ref[b, k] = high
            low_ref[b, k] = (now[b] - high.astype(jnp.float32)).astype(jnp.bfloat16)
            if k + 1 < LAYERS:
                now[b] = product(
                    now[b] * rate_ref[:, pl.ds(b * BLK, BLK)], high_ref[b, 0], low_ref[b, 0]
                )


def product(face, high, low):
    top = face.astype(jnp.bfloat16)
    rest = (face - top.astype(jnp.float32)).astype(jnp.bfloat16)
    rows = face.shape[0]
    both = jnp.dot(
        jnp.concatenate([top, rest], axis=0), high, preferred_element_type=jnp.float32
    )
    return both[:rows] + both[rows:] + jnp.dot(top, low, preferred_element_type=jnp.float32)


def last_kernel(direction_ref, *refs):
    halves, wholes, quarters = refs[:8], refs[8:10], refs[10:12]
    high_ref, low_ref, source_ref, out_ref = refs[12:]
    for side in range(2):
        rows = pl.ds(side * HALF, HALF)
        total = quarters[side][...]
        for part in halves[4 * side : 4 * side + 4]:
            total += part[...]
        for part in wholes:
            total += part[rows, :]
        source_ref[rows, :] = total
    for b in range(SHELL):
        lanes = pl.ds(b * BLK, BLK)
        up = direction_ref[b] == 1
        total = jnp.zeros((LATERAL, BLK), jnp.float32)
        for t in range(LAYERS):
            k = jnp.where(up, LAYERS - 1 - t, t)
            total += product(
                source_ref[pl.ds(t * LATERAL, LATERAL), lanes], high_ref[b, k], low_ref[b, k]
            )
        out_ref[:, lanes] = total


def particular_kernel(direction_ref, source_ref, rate_ref, high_ref, low_ref, out_ref):
    now = [jnp.zeros((LATERAL, BLK), jnp.float32) for _ in range(SHELL)]
    for t in range(LAYERS):
        for b in range(SHELL):
            lanes = pl.ds(b * BLK, BLK)
            at = jnp.where(direction_ref[b] == 1, t, LAYERS - 1 - t)
            rows = pl.ds(pl.multiple_of(at * LATERAL, LATERAL), LATERAL)
            now[b] = product(
                source_ref[rows, lanes] + rate_ref[:, lanes] * now[b], high_ref[b, 0], low_ref[b, 0]
            )
            out_ref[rows, lanes] = now[b]


def finish_kernel(
    direction_ref,
    slab_ref,
    wall_ref,
    one_ref,
    two_ref,
    three_ref,
    rate_ref,
    particular_ref,
    high_ref,
    low_ref,
    out_ref,
    faces,
):
    for k, face in enumerate((one_ref, two_ref, three_ref)):
        faces[k] = face[...]
    slab = slab_ref[0]
    now = [wall_ref[:, pl.ds(b * BLK, BLK)] for b in range(SHELL)]
    for n in range(3):
        for b in range(SHELL):
            lanes = pl.ds(b * BLK, BLK)
            up = direction_ref[b] == 1
            k = jnp.where(up, 2 - n, n)
            active = jnp.where(
                up, (k + 1 <= slab).astype(jnp.int32), (k + 1 > slab).astype(jnp.int32)
            )
            moved = faces[k, :, lanes] + product(
                now[b] * rate_ref[:, lanes], high_ref[b, LAYERS - 1], low_ref[b, LAYERS - 1]
            )
            now[b] = jnp.where(active == 1, moved, now[b])
    for b in range(SHELL):
        lanes = pl.ds(b * BLK, BLK)
        up = direction_ref[b] == 1
        scaled = now[b] * rate_ref[:, lanes]
        for t in range(LAYERS):
            k = jnp.where(up, t, LAYERS - 1 - t)
            rows = pl.ds(t * LATERAL, LATERAL)
            out_ref[rows, lanes] = particular_ref[rows, lanes] + product(
                scaled, high_ref[b, k], low_ref[b, k]
            )


SMEM = pl.BlockSpec(memory_space=pltpu.SMEM)
VMEM = pl.BlockSpec(memory_space=pltpu.VMEM)


def small_call(kernel, outs, specs, scratch=(), flops=0, name=None):
    return pl.pallas_call(
        kernel,
        in_specs=specs,
        out_specs=[VMEM] * len(outs),
        out_shape=[jax.ShapeDtypeStruct(*out) for out in outs],
        scratch_shapes=list(scratch),
        cost_estimate=pl.CostEstimate(flops=flops, bytes_accessed=3 << 20, transcendentals=0),
        name=name,
    )


def per_device(
    occupation_prior,
    coupling,
    pattern,
    pseudo_weights,
    equilibrium_slope,
    direction,
    stream_rate,
    inscatter,
    inflow_low,
    inflow_high,
    front_of_row,
):
    modes = lax.axis_index("modes").astype(jnp.int32)
    slab = lax.axis_index("slab").astype(jnp.int32)
    here = (modes // (SIDE * SIDE), modes // SIDE % SIDE, modes % SIDE)
    weights = pseudo_weights.reshape(1, WIDTH)
    rate = stream_rate.reshape(1, WIDTH)
    slope = equilibrium_slope.reshape(SIDE**3, 1, WIDTH)
    make = functools.partial(
        partial_sums,
        groups=group_table(here),
        pattern=pattern,
        prior=occupation_prior,
        weights=weights,
        slope=slope,
        coupling=coupling,
    )
    pairs = (UPPER, UPPER, LOWER, LOWER)
    def ring(blocks, step):
        axes = (2, 2, 1, 1)
        signs = (step, -step, step, -step)
        return [send(block, axis, sign) for block, axis, sign in zip(blocks, axes, signs)]

    def spread(blocks, axis):
        return [send(block, axis, step) for block, step in zip(blocks, (1, 2, -1))]

    far_got = ring(make(pairs, 0, 2, ()), 1)
    early = ring(make(pairs, 8, 2, ()), -1)
    late = ring(make(pairs, 16, 2, far_got), 1)
    kept = make(pairs, 24, 2, early)
    near = make((((0, HALF, 0),),) * SIDE + (((HALF, HALF, 0),),) * SIDE, 32, SIDE, ())
    rows = [
        (kept[c][i] + late[c][i], kept[c + 1][i] + late[c + 1][i])
        for c in (0, 2)
        for i in (0, 1)
    ]
    a0, a2, a1, a3 = rows[0] + rows[1]
    b0, b2, b1, b3 = rows[2] + rows[3]
    (a1, a2, a3, b1, b2, b3), near = lax.optimization_barrier(((a1, a2, a3, b1, b2, b3), near))
    a_got = spread((a1, a2, a3), 1)
    b_got = spread((b1, b2, b3), 2)
    near_a = spread(near[1:4], 2)
    near_b = spread(near[5:8], 1)
    a_sum = a0 + a_got[0] + a_got[1] + a_got[2]
    b_sum = b0 + b_got[0] + b_got[1] + b_got[2]
    from_below = send(a_sum[:CELL], 0, 1)
    far_a = send(a_sum[CELL:], 0, 2)
    from_above = send(b_sum[:CELL], 0, -1)
    far_b = send(b_sum[CELL:], 0, 2)

    def ends(own, got, axis):
        parts = [own[i] + got[0][i] + got[1][i] + got[2][i] for i in range(SIDE)]
        return [parts[0]] + spread(parts[1:], axis)

    halves = ends(near[0], near_a, 1) + ends(near[4], near_b, 2)

    split = [((SHELL, LAYERS, BLK, BLK), jnp.bfloat16)] * 2
    high, low = small_call(powers_kernel, split, [VMEM, VMEM], flops=200_000_000, name="powers")(
        rate, inscatter
    )
    picks = front_of_row[:, None] == jnp.arange(inflow_low.shape[0], dtype=jnp.int32)[None, :]
    ahead = (jnp.repeat(direction, BLK) == 1)[None, :]
    inflow = jnp.where(ahead, inflow_low, inflow_high)
    wall = jnp.sum(jnp.where(picks[:, :, None], inflow[None, :, :], 0.0), axis=1)

    whole = ((CELL, WIDTH), jnp.float32)
    source, last = small_call(
        last_kernel,
        [whole, ((LATERAL, WIDTH), jnp.float32)],
        [SMEM] + [VMEM] * 14,
        flops=40_000_000,
        name="last_face",
    )(direction, *halves, from_below, from_above, far_a, far_b, high, low)
    faces = [
        lax.ppermute(last, "slab", [(i, (i + k) % 4) for i in range(4)]) for k in (1, 2, 3)
    ]
    (particular,) = small_call(
        particular_kernel, [whole], [SMEM] + [VMEM] * 4, flops=40_000_000, name="particular"
    )(direction, source, rate, high, low)
    (swept,) = small_call(
        finish_kernel,
        [whole],
        [SMEM, SMEM] + [VMEM] * 8,
        scratch=[pltpu.VMEM((3, LATERAL, WIDTH), jnp.float32)],
        flops=60_000_000,
        name="finish",
    )(direction, slab.reshape(1), wall, *faces, rate, particular, high, low)
    return swept


def solution(mesh):
    placed = (
        P("slab", "modes"),
        P("modes", None, None, None),
        P("modes", None),
        P("modes"),
        P(),
        P("modes"),
        P("modes"),
        P("modes", None, None),
        P(None, "modes"),
        P(None, "modes"),
        P(),
    )
    return jax.shard_map(
        per_device, mesh=mesh, in_specs=placed, out_specs=P("slab", "modes"), check_vma=False
    )
```

```python
import functools

import jax
import jax.numpy as jnp
from jax import lax
from jax.experimental import pallas as pl
from jax.experimental.pallas import tpu as pltpu
from jax.sharding import PartitionSpec as P


BLK = 128
SHELL = 4
SIDE = 4
LAYERS = 8
LATERAL = 16
WIDTH = SHELL * BLK
CELL = LAYERS * LATERAL
HALF = CELL // 2


def route(axis, step):
    pairs = []
    for z in range(SIDE):
        for y in range(SIDE):
            for x in range(SIDE):
                there = [z, y, x]
                there[axis] = (there[axis] + step) % SIDE
                pairs.append(
                    ((z * SIDE + y) * SIDE + x, (there[0] * SIDE + there[1]) * SIDE + there[2])
                )
    return pairs


def send(block, axis, step):
    return lax.ppermute(block, "modes", route(axis, step))


def target(segment, place, i):
    _, _, z_step, upper, pair, step = segment
    along = pair + i
    y, x = (along, step) if upper else (step, along)
    z = ((place >> 4) + z_step) & 3
    return z * 16 + (((place >> 2) + y) & 3) * 4 + ((place + x) & 3)


def partial_kernel(jobs, addends, place_ref, pattern_ref, x_ref, weight_ref, *refs):
    segments = sum(len(job) for job in jobs)
    slopes, couplings = refs[:segments], refs[segments : 2 * segments]
    refs = refs[2 * segments :]
    added, outs = refs[:addends], refs[addends : addends + len(jobs)]
    rounded, warmth = refs[addends + len(jobs) :]
    step = pl.program_id(0)

    @pl.when(step == 0)
    def _():
        prior = x_ref[...]
        rounded[...] = prior.astype(jnp.bfloat16)
        total = jnp.sum(prior * weight_ref[...], axis=1, keepdims=True)
        warmth[...] = jnp.broadcast_to(total, warmth.shape)

    n = 0
    for index, job in enumerate(jobs):
        out_ref = outs[index]
        base = 0
        for segment in job:
            from_row, count = segment[:2]
            cells = pl.ds(from_row, count)
            rows = pl.ds(base, count)
            group = target(segment, place_ref[0], step)
            heat = warmth[cells, :]
            for t in range(SHELL):
                lanes = pl.ds(t * BLK, BLK)
                start = heat * slopes[n][0, :, lanes]
                if addends:
                    start += added[index][0, rows, lanes]
                out_ref[0, rows, lanes] = start
            for b in range(SHELL):
                product = jnp.dot(
                    rounded[cells, pl.ds(b * BLK, BLK)],
                    couplings[n][b, 0],
                    preferred_element_type=jnp.float32,
                )
                where = pattern_ref[b, group]
                lanes = pl.ds(pl.multiple_of(where * BLK, BLK), BLK)
                out_ref[0, rows, lanes] += product
            base += count
            n += 1


def partial_sums(jobs, units, addends, place, pattern, prior, weights, slope, coupling):
    segments = [segment for job in jobs for segment in job]
    slope_specs = [
        pl.BlockSpec(
            (1, 1, WIDTH), functools.partial(lambda n, i, m, p: (target(n, m[0], i), 0, 0), n)
        )
        for n in segments
    ]
    coupling_specs = [
        pl.BlockSpec(
            (SHELL, 1, BLK, BLK),
            functools.partial(lambda n, i, m, p: (0, target(n, m[0], i), 0, 0), n),
        )
        for n in segments
    ]
    heights = [sum(segment[1] for segment in job) for job in jobs]
    blocks = [pl.BlockSpec((1, rows, WIDTH), lambda i, g, p: (i, 0, 0)) for rows in heights]
    return pl.pallas_call(
        functools.partial(partial_kernel, jobs, len(addends)),
        grid_spec=pltpu.PrefetchScalarGridSpec(
            num_scalar_prefetch=2,
            grid=(units,),
            in_specs=[
                pl.BlockSpec((CELL, WIDTH), lambda i, g, p: (0, 0)),
                pl.BlockSpec((1, WIDTH), lambda i, g, p: (0, 0)),
            ]
            + slope_specs
            + coupling_specs
            + blocks[: len(addends)],
            out_specs=blocks,
            scratch_shapes=[
                pltpu.VMEM((CELL, WIDTH), jnp.bfloat16),
                pltpu.VMEM((CELL, BLK), jnp.float32),
            ],
        ),
        out_shape=[jax.ShapeDtypeStruct((units, rows, WIDTH), jnp.float32) for rows in heights],
        cost_estimate=pl.CostEstimate(
            flops=2 * sum(heights) * units * WIDTH * BLK,
            bytes_accessed=sum(heights) * units * WIDTH * 6,
            transcendentals=0,
        ),
        name="partial_sums",
    )(
        place,
        pattern,
        prior,
        weights,
        *([slope] * len(segments)),
        *([coupling] * len(segments)),
        *addends,
    )


def powers_kernel(rate_ref, inscatter_ref, high_ref, low_ref):
    row = lax.broadcasted_iota(jnp.int32, (BLK, BLK), 0)
    column = lax.broadcasted_iota(jnp.int32, (BLK, BLK), 1)
    unit = jnp.where(row == column, 1.0, 0.0).astype(jnp.float32)
    now = [unit + inscatter_ref[b] for b in range(SHELL)]
    for k in range(LAYERS):
        for b in range(SHELL):
            high = now[b].astype(jnp.bfloat16)
            high_ref[b, k] = high
            low_ref[b, k] = (now[b] - high.astype(jnp.float32)).astype(jnp.bfloat16)
            if k + 1 < LAYERS:
                now[b] = product(
                    now[b] * rate_ref[:, pl.ds(b * BLK, BLK)], high_ref[b, 0], low_ref[b, 0]
                )


def product(face, high, low):
    top = face.astype(jnp.bfloat16)
    rest = (face - top.astype(jnp.float32)).astype(jnp.bfloat16)
    rows = face.shape[0]
    both = jnp.dot(
        jnp.concatenate([top, rest], axis=0), high, preferred_element_type=jnp.float32
    )
    return both[:rows] + both[rows:] + jnp.dot(top, low, preferred_element_type=jnp.float32)


def last_kernel(direction_ref, *refs):
    halves, wholes, quarters = refs[:8], refs[8:10], refs[10:12]
    high_ref, low_ref, source_ref, out_ref = refs[12:]
    for side in range(2):
        rows = pl.ds(side * HALF, HALF)
        total = quarters[side][...]
        for part in halves[4 * side : 4 * side + 4]:
            total += part[...]
        for part in wholes:
            total += part[rows, :]
        source_ref[rows, :] = total
    for b in range(SHELL):
        lanes = pl.ds(b * BLK, BLK)
        up = direction_ref[b] == 1
        total = jnp.zeros((LATERAL, BLK), jnp.float32)
        for t in range(LAYERS):
            k = jnp.where(up, LAYERS - 1 - t, t)
            total += product(
                source_ref[pl.ds(t * LATERAL, LATERAL), lanes], high_ref[b, k], low_ref[b, k]
            )
        out_ref[:, lanes] = total


def particular_kernel(direction_ref, source_ref, rate_ref, high_ref, low_ref, out_ref):
    now = [jnp.zeros((LATERAL, BLK), jnp.float32) for _ in range(SHELL)]
    for t in range(LAYERS):
        for b in range(SHELL):
            lanes = pl.ds(b * BLK, BLK)
            at = jnp.where(direction_ref[b] == 1, t, LAYERS - 1 - t)
            rows = pl.ds(pl.multiple_of(at * LATERAL, LATERAL), LATERAL)
            now[b] = product(
                source_ref[rows, lanes] + rate_ref[:, lanes] * now[b], high_ref[b, 0], low_ref[b, 0]
            )
            out_ref[rows, lanes] = now[b]


def finish_kernel(
    direction_ref,
    slab_ref,
    wall_ref,
    one_ref,
    two_ref,
    three_ref,
    rate_ref,
    particular_ref,
    high_ref,
    low_ref,
    out_ref,
    faces,
):
    for k, face in enumerate((one_ref, two_ref, three_ref)):
        faces[k] = face[...]
    slab = slab_ref[0]
    now = [wall_ref[:, pl.ds(b * BLK, BLK)] for b in range(SHELL)]
    for n in range(3):
        for b in range(SHELL):
            lanes = pl.ds(b * BLK, BLK)
            up = direction_ref[b] == 1
            k = jnp.where(up, 2 - n, n)
            active = jnp.where(
                up, (k + 1 <= slab).astype(jnp.int32), (k + 1 > slab).astype(jnp.int32)
            )
            moved = faces[k, :, lanes] + product(
                now[b] * rate_ref[:, lanes], high_ref[b, LAYERS - 1], low_ref[b, LAYERS - 1]
            )
            now[b] = jnp.where(active == 1, moved, now[b])
    for b in range(SHELL):
        lanes = pl.ds(b * BLK, BLK)
        up = direction_ref[b] == 1
        scaled = now[b] * rate_ref[:, lanes]
        for t in range(LAYERS):
            k = jnp.where(up, t, LAYERS - 1 - t)
            rows = pl.ds(t * LATERAL, LATERAL)
            out_ref[rows, lanes] = particular_ref[rows, lanes] + product(
                scaled, high_ref[b, k], low_ref[b, k]
            )


SMEM = pl.BlockSpec(memory_space=pltpu.SMEM)
VMEM = pl.BlockSpec(memory_space=pltpu.VMEM)


def small_call(kernel, outs, specs, scratch=(), flops=0):
    return pl.pallas_call(
        kernel,
        in_specs=specs,
        out_specs=[VMEM] * len(outs),
        out_shape=[jax.ShapeDtypeStruct(*out) for out in outs],
        scratch_shapes=list(scratch),
        cost_estimate=pl.CostEstimate(flops=flops, bytes_accessed=3 << 20, transcendentals=0),
    )


def per_device(
    occupation_prior,
    coupling,
    pattern,
    pseudo_weights,
    equilibrium_slope,
    direction,
    stream_rate,
    inscatter,
    inflow_low,
    inflow_high,
    front_of_row,
):
    modes = lax.axis_index("modes").astype(jnp.int32)
    slab = lax.axis_index("slab").astype(jnp.int32)
    weights = pseudo_weights.reshape(1, WIDTH)
    rate = stream_rate.reshape(1, WIDTH)
    slope = equilibrium_slope.reshape(SIDE**3, 1, WIDTH)
    make = functools.partial(
        partial_sums,
        place=modes.reshape(1),
        pattern=pattern,
        weights=weights,
        slope=slope,
        coupling=coupling,
    )

    def ring_sums(low_step, high_step, prior, addends=()):
        jobs = [
            (
                (0, CELL, 1 if upper else 3, upper, pair, step),
                (0 if upper else HALF, HALF, 2, upper, pair, step),
            )
            for upper in (True, False)
            for pair, step in ((0, low_step), (2, high_step))
        ]
        return make(tuple(jobs), 2, addends, prior=prior)

    def ring(blocks, step):
        axes = (2, 2, 1, 1)
        signs = (step, -step, step, -step)
        moved = []
        for index, block in enumerate(blocks):
            moved.append(send(block, axes[index], signs[index]))
        return moved

    def spread(blocks, axis):
        return [send(block, axis, step) for block, step in zip(blocks, (1, 2, -1))]

    prior = occupation_prior
    split = [((SHELL, LAYERS, BLK, BLK), jnp.bfloat16)] * 2
    high, low = small_call(powers_kernel, split, [VMEM, VMEM], flops=200_000_000)(rate, inscatter)
    picks = front_of_row[:, None] == jnp.arange(inflow_low.shape[0], dtype=jnp.int32)[None, :]
    ahead = (jnp.repeat(direction, BLK) == 1)[None, :]
    inflow = jnp.where(ahead, inflow_low, inflow_high)
    wall = jnp.sum(jnp.where(picks[:, :, None], inflow[None, :, :], 0.0), axis=1)

    far_got = ring(ring_sums(2, 2, prior), 1)
    direct = ring_sums(3, 1, prior)
    early = ring(direct, -1)
    after, _ = lax.optimization_barrier((prior, direct))
    near = make(
        tuple(
            ((0 if upper else HALF, HALF, 0, upper, 0, step),)
            for upper in (True, False)
            for step in range(SIDE)
        ),
        SIDE,
        (),
        prior=after,
    )
    far_got, near = lax.optimization_barrier((far_got, near))
    late = ring(ring_sums(1, 3, prior, far_got), 1)
    early, high, low, wall = lax.optimization_barrier((early, high, low, wall))
    kept = ring_sums(0, 0, prior, early)
    a1, a3, a2 = kept[0][1] + late[0][1], kept[1][1] + late[1][1], kept[1][0] + late[1][0]
    b1, b3, b2 = kept[2][1] + late[2][1], kept[3][1] + late[3][1], kept[3][0] + late[3][0]
    near, _ = lax.optimization_barrier((near, (a1, a2, a3, b1, b2, b3)))
    a_got = spread((a1, a2, a3), 1)
    b_got = spread((b1, b2, b3), 2)
    near_a = spread(near[1:4], 2)
    near_b = spread(near[5:8], 1)
    a_own, b_own, a_got, b_got = lax.optimization_barrier(
        ((kept[0], late[0]), (kept[2], late[2]), a_got, b_got)
    )
    a_sum = a_own[0][0] + a_own[1][0] + a_got[0] + a_got[1] + a_got[2]
    b_sum = b_own[0][0] + b_own[1][0] + b_got[0] + b_got[1] + b_got[2]
    from_below = send(a_sum[:CELL], 0, 1)
    far_a = send(a_sum[CELL:], 0, 2)
    from_above = send(b_sum[:CELL], 0, -1)
    far_b = send(b_sum[CELL:], 0, 2)

    def ends(own, got, axis):
        parts = [own[i] + got[0][i] + got[1][i] + got[2][i] for i in range(SIDE)]
        return [parts[0]] + spread(parts[1:], axis)

    halves = ends(near[0], near_a, 1) + ends(near[4], near_b, 2)

    whole = ((CELL, WIDTH), jnp.float32)
    source, last = small_call(
        last_kernel,
        [whole, ((LATERAL, WIDTH), jnp.float32)],
        [SMEM] + [VMEM] * 14,
        flops=40_000_000,
    )(direction, *halves, from_below, from_above, far_a, far_b, high, low)
    faces = [
        lax.ppermute(last, "slab", [(i, (i + k) % 4) for i in range(4)]) for k in (1, 2, 3)
    ]
    (particular,) = small_call(
        particular_kernel, [whole], [SMEM] + [VMEM] * 4, flops=40_000_000
    )(direction, source, rate, high, low)
    (swept,) = small_call(
        finish_kernel,
        [whole],
        [SMEM, SMEM] + [VMEM] * 8,
        scratch=[pltpu.VMEM((3, LATERAL, WIDTH), jnp.float32)],
        flops=60_000_000,
    )(direction, slab.reshape(1), wall, *faces, rate, particular, high, low)
    return swept


def solution(mesh):
    placed = (
        P("slab", "modes"),
        P("modes", None, None, None),
        P("modes", None),
        P("modes"),
        P(),
        P("modes"),
        P("modes"),
        P("modes", None, None),
        P(None, "modes"),
        P(None, "modes"),
        P(),
    )

    return jax.shard_map(
        per_device, mesh=mesh, in_specs=placed, out_specs=P("slab", "modes"), check_vma=False
    )
```

```python
import functools

import jax
import jax.numpy as jnp
from jax import lax
from jax.experimental import pallas as pl
from jax.experimental.pallas import tpu as pltpu
from jax.sharding import PartitionSpec as P


BLK = 128
SHELL = 4
SIDE = 4
LAYERS = 8
LATERAL = 16
WIDTH = SHELL * BLK
CELL = LAYERS * LATERAL
HALF = CELL // 2


def route(axis, step):
    pairs = []
    for z in range(SIDE):
        for y in range(SIDE):
            for x in range(SIDE):
                there = [z, y, x]
                there[axis] = (there[axis] + step) % SIDE
                pairs.append(
                    ((z * SIDE + y) * SIDE + x, (there[0] * SIDE + there[1]) * SIDE + there[2])
                )
    return pairs


def send(block, axis, step):
    return lax.ppermute(block, "modes", route(axis, step))


def target(segment, place, i):
    _, _, z_step, upper, pair, step = segment
    along = pair + i
    y, x = (along, step) if upper else (step, along)
    z = ((place >> 4) + z_step) & 3
    return z * 16 + (((place >> 2) + y) & 3) * 4 + ((place + x) & 3)


def partial_kernel(jobs, addends, place_ref, pattern_ref, x_ref, weight_ref, *refs):
    segments = sum(len(job) for job in jobs)
    slopes, couplings = refs[:segments], refs[segments : 2 * segments]
    refs = refs[2 * segments :]
    added, outs = refs[:addends], refs[addends : addends + len(jobs)]
    rounded, warmth = refs[addends + len(jobs) :]
    step = pl.program_id(0)

    @pl.when(step == 0)
    def _():
        prior = x_ref[...]
        rounded[...] = prior.astype(jnp.bfloat16)
        total = jnp.sum(prior * weight_ref[...], axis=1, keepdims=True)
        warmth[...] = jnp.broadcast_to(total, warmth.shape)

    n = 0
    for index, job in enumerate(jobs):
        out_ref = outs[index]
        base = 0
        for segment in job:
            from_row, count = segment[:2]
            cells = pl.ds(from_row, count)
            rows = pl.ds(base, count)
            group = target(segment, place_ref[0], step)
            heat = warmth[cells, :]
            for t in range(SHELL):
                lanes = pl.ds(t * BLK, BLK)
                start = heat * slopes[n][0, :, lanes]
                if addends:
                    start += added[index][0, rows, lanes]
                out_ref[0, rows, lanes] = start
            for b in range(SHELL):
                product = jnp.dot(
                    rounded[cells, pl.ds(b * BLK, BLK)],
                    couplings[n][b, 0],
                    preferred_element_type=jnp.float32,
                )
                where = pattern_ref[b, group]
                lanes = pl.ds(pl.multiple_of(where * BLK, BLK), BLK)
                out_ref[0, rows, lanes] += product
            base += count
            n += 1


def partial_sums(jobs, units, addends, place, pattern, prior, weights, slope, coupling):
    segments = [segment for job in jobs for segment in job]
    slope_specs = [
        pl.BlockSpec(
            (1, 1, WIDTH), functools.partial(lambda n, i, m, p: (target(n, m[0], i), 0, 0), n)
        )
        for n in segments
    ]
    coupling_specs = [
        pl.BlockSpec(
            (SHELL, 1, BLK, BLK),
            functools.partial(lambda n, i, m, p: (0, target(n, m[0], i), 0, 0), n),
        )
        for n in segments
    ]
    heights = [sum(segment[1] for segment in job) for job in jobs]
    blocks = [pl.BlockSpec((1, rows, WIDTH), lambda i, g, p: (i, 0, 0)) for rows in heights]
    return pl.pallas_call(
        functools.partial(partial_kernel, jobs, len(addends)),
        grid_spec=pltpu.PrefetchScalarGridSpec(
            num_scalar_prefetch=2,
            grid=(units,),
            in_specs=[
                pl.BlockSpec((CELL, WIDTH), lambda i, g, p: (0, 0)),
                pl.BlockSpec((1, WIDTH), lambda i, g, p: (0, 0)),
            ]
            + slope_specs
            + coupling_specs
            + blocks[: len(addends)],
            out_specs=blocks,
            scratch_shapes=[
                pltpu.VMEM((CELL, WIDTH), jnp.bfloat16),
                pltpu.VMEM((CELL, BLK), jnp.float32),
            ],
        ),
        out_shape=[jax.ShapeDtypeStruct((units, rows, WIDTH), jnp.float32) for rows in heights],
        cost_estimate=pl.CostEstimate(
            flops=2 * sum(heights) * units * WIDTH * BLK,
            bytes_accessed=sum(heights) * units * WIDTH * 6,
            transcendentals=0,
        ),
        name="partial_sums",
    )(
        place,
        pattern,
        prior,
        weights,
        *([slope] * len(segments)),
        *([coupling] * len(segments)),
        *addends,
    )


def powers_kernel(rate_ref, inscatter_ref, high_ref, low_ref):
    row = lax.broadcasted_iota(jnp.int32, (BLK, BLK), 0)
    column = lax.broadcasted_iota(jnp.int32, (BLK, BLK), 1)
    unit = jnp.where(row == column, 1.0, 0.0).astype(jnp.float32)
    now = [unit + inscatter_ref[b] for b in range(SHELL)]
    for k in range(LAYERS):
        for b in range(SHELL):
            high = now[b].astype(jnp.bfloat16)
            high_ref[b, k] = high
            low_ref[b, k] = (now[b] - high.astype(jnp.float32)).astype(jnp.bfloat16)
            if k + 1 < LAYERS:
                now[b] = product(
                    now[b] * rate_ref[:, pl.ds(b * BLK, BLK)], high_ref[b, 0], low_ref[b, 0]
                )


def product(face, high, low):
    top = face.astype(jnp.bfloat16)
    rest = (face - top.astype(jnp.float32)).astype(jnp.bfloat16)
    rows = face.shape[0]
    both = jnp.dot(
        jnp.concatenate([top, rest], axis=0), high, preferred_element_type=jnp.float32
    )
    return both[:rows] + both[rows:] + jnp.dot(top, low, preferred_element_type=jnp.float32)


def last_kernel(direction_ref, *refs):
    halves, wholes, quarters = refs[:8], refs[8:10], refs[10:12]
    high_ref, low_ref, source_ref, out_ref = refs[12:]
    for side in range(2):
        rows = pl.ds(side * HALF, HALF)
        total = quarters[side][...]
        for part in halves[4 * side : 4 * side + 4]:
            total += part[...]
        for part in wholes:
            total += part[rows, :]
        source_ref[rows, :] = total
    for b in range(SHELL):
        lanes = pl.ds(b * BLK, BLK)
        up = direction_ref[b] == 1
        total = jnp.zeros((LATERAL, BLK), jnp.float32)
        for t in range(LAYERS):
            k = jnp.where(up, LAYERS - 1 - t, t)
            total += product(
                source_ref[pl.ds(t * LATERAL, LATERAL), lanes], high_ref[b, k], low_ref[b, k]
            )
        out_ref[:, lanes] = total


def particular_kernel(direction_ref, source_ref, rate_ref, high_ref, low_ref, out_ref):
    now = [jnp.zeros((LATERAL, BLK), jnp.float32) for _ in range(SHELL)]
    for t in range(LAYERS):
        for b in range(SHELL):
            lanes = pl.ds(b * BLK, BLK)
            at = jnp.where(direction_ref[b] == 1, t, LAYERS - 1 - t)
            rows = pl.ds(pl.multiple_of(at * LATERAL, LATERAL), LATERAL)
            now[b] = product(
                source_ref[rows, lanes] + rate_ref[:, lanes] * now[b], high_ref[b, 0], low_ref[b, 0]
            )
            out_ref[rows, lanes] = now[b]


def finish_kernel(
    direction_ref,
    slab_ref,
    wall_ref,
    one_ref,
    two_ref,
    three_ref,
    rate_ref,
    particular_ref,
    high_ref,
    low_ref,
    out_ref,
    faces,
):
    for k, face in enumerate((one_ref, two_ref, three_ref)):
        faces[k] = face[...]
    slab = slab_ref[0]
    now = [wall_ref[:, pl.ds(b * BLK, BLK)] for b in range(SHELL)]
    for n in range(3):
        for b in range(SHELL):
            lanes = pl.ds(b * BLK, BLK)
            up = direction_ref[b] == 1
            k = jnp.where(up, 2 - n, n)
            active = jnp.where(
                up, (k + 1 <= slab).astype(jnp.int32), (k + 1 > slab).astype(jnp.int32)
            )
            moved = faces[k, :, lanes] + product(
                now[b] * rate_ref[:, lanes], high_ref[b, LAYERS - 1], low_ref[b, LAYERS - 1]
            )
            now[b] = jnp.where(active == 1, moved, now[b])
    for b in range(SHELL):
        lanes = pl.ds(b * BLK, BLK)
        up = direction_ref[b] == 1
        scaled = now[b] * rate_ref[:, lanes]
        for t in range(LAYERS):
            k = jnp.where(up, t, LAYERS - 1 - t)
            rows = pl.ds(t * LATERAL, LATERAL)
            out_ref[rows, lanes] = particular_ref[rows, lanes] + product(
                scaled, high_ref[b, k], low_ref[b, k]
            )


SMEM = pl.BlockSpec(memory_space=pltpu.SMEM)
VMEM = pl.BlockSpec(memory_space=pltpu.VMEM)


def small_call(kernel, outs, specs, scratch=(), flops=0):
    return pl.pallas_call(
        kernel,
        in_specs=specs,
        out_specs=[VMEM] * len(outs),
        out_shape=[jax.ShapeDtypeStruct(*out) for out in outs],
        scratch_shapes=list(scratch),
        cost_estimate=pl.CostEstimate(flops=flops, bytes_accessed=3 << 20, transcendentals=0),
    )


def per_device(
    occupation_prior,
    coupling,
    pattern,
    pseudo_weights,
    equilibrium_slope,
    direction,
    stream_rate,
    inscatter,
    inflow_low,
    inflow_high,
    front_of_row,
):
    modes = lax.axis_index("modes").astype(jnp.int32)
    slab = lax.axis_index("slab").astype(jnp.int32)
    weights = pseudo_weights.reshape(1, WIDTH)
    rate = stream_rate.reshape(1, WIDTH)
    slope = equilibrium_slope.reshape(SIDE**3, 1, WIDTH)
    make = functools.partial(
        partial_sums,
        place=modes.reshape(1),
        pattern=pattern,
        weights=weights,
        slope=slope,
        coupling=coupling,
    )

    def ring_sums(low_step, high_step, prior, addends=()):
        jobs = [
            (
                (0, CELL, 1 if upper else 3, upper, pair, step),
                (0 if upper else HALF, HALF, 2, upper, pair, step),
            )
            for upper in (True, False)
            for pair, step in ((0, low_step), (2, high_step))
        ]
        return make(tuple(jobs), 2, addends, prior=prior)

    def ring(blocks, step):
        axes = (2, 2, 1, 1)
        signs = (step, -step, step, -step)
        moved = []
        for index, block in enumerate(blocks):
            moved.append(send(block, axes[index], signs[index]))
        return moved

    def spread(blocks, axis):
        return [send(block, axis, step) for block, step in zip(blocks, (1, 2, -1))]

    prior = occupation_prior
    split = [((SHELL, LAYERS, BLK, BLK), jnp.bfloat16)] * 2
    high, low = small_call(powers_kernel, split, [VMEM, VMEM], flops=200_000_000)(rate, inscatter)
    picks = front_of_row[:, None] == jnp.arange(inflow_low.shape[0], dtype=jnp.int32)[None, :]
    ahead = (jnp.repeat(direction, BLK) == 1)[None, :]
    inflow = jnp.where(ahead, inflow_low, inflow_high)
    wall = jnp.sum(jnp.where(picks[:, :, None], inflow[None, :, :], 0.0), axis=1)

    far_got = ring(ring_sums(2, 2, prior), 1)
    direct = ring_sums(3, 1, prior)
    early = ring(direct, -1)
    after, _ = lax.optimization_barrier((prior, direct))
    near = make(
        tuple(
            ((0 if upper else HALF, HALF, 0, upper, 0, step),)
            for upper in (True, False)
            for step in range(SIDE)
        ),
        SIDE,
        (),
        prior=after,
    )
    far_got, near = lax.optimization_barrier((far_got, near))
    beside = ((near[1], 2, 1), (near[3], 2, -1), (near[5], 1, 1), (near[7], 1, -1))
    late = ring(ring_sums(1, 3, prior, far_got), 1)
    early, high, low, wall = lax.optimization_barrier((early, high, low, wall))
    kept = ring_sums(0, 0, prior, early)
    a1, a3, a2 = kept[0][1] + late[0][1], kept[1][1] + late[1][1], kept[1][0] + late[1][0]
    b1, b3, b2 = kept[2][1] + late[2][1], kept[3][1] + late[3][1], kept[3][0] + late[3][0]
    near_got = []
    for block, axis, step in beside:
        near_got.append(send(block, axis, step))
    across, _ = lax.optimization_barrier(((near[2], near[6]), (a1, a2, a3, b1, b2, b3)))
    a_got = spread((a1, a2, a3), 1)
    b_got = spread((b1, b2, b3), 2)
    near_a = [near_got[0], near_got[1], send(across[0], 2, 2)]
    near_b = [near_got[2], near_got[3], send(across[1], 1, 2)]
    a_own, a_got = lax.optimization_barrier(((kept[0], late[0]), a_got))
    b_own, b_got = lax.optimization_barrier(((kept[2], late[2]), b_got))
    a_sum = a_own[0][0] + a_own[1][0] + a_got[0] + a_got[1] + a_got[2]
    b_sum = b_own[0][0] + b_own[1][0] + b_got[0] + b_got[1] + b_got[2]
    from_below = send(a_sum[:CELL], 0, 1)
    far_a = send(a_sum[CELL:], 0, 2)
    from_above = send(b_sum[:CELL], 0, -1)
    far_b = send(b_sum[CELL:], 0, 2)

    def ends(own, got, axis):
        parts = [own[i] + got[0][i] + got[1][i] + got[2][i] for i in range(SIDE)]
        return [parts[0]] + spread(parts[1:], axis)

    halves = ends(near[0], near_a, 1) + ends(near[4], near_b, 2)

    whole = ((CELL, WIDTH), jnp.float32)
    source, last = small_call(
        last_kernel,
        [whole, ((LATERAL, WIDTH), jnp.float32)],
        [SMEM] + [VMEM] * 14,
        flops=40_000_000,
    )(direction, *halves, from_below, from_above, far_a, far_b, high, low)
    faces = [
        lax.ppermute(last, "slab", [(i, (i + k) % 4) for i in range(4)]) for k in (1, 2, 3)
    ]
    (particular,) = small_call(
        particular_kernel, [whole], [SMEM] + [VMEM] * 4, flops=40_000_000
    )(direction, source, rate, high, low)
    (swept,) = small_call(
        finish_kernel,
        [whole],
        [SMEM, SMEM] + [VMEM] * 8,
        scratch=[pltpu.VMEM((3, LATERAL, WIDTH), jnp.float32)],
        flops=60_000_000,
    )(direction, slab.reshape(1), wall, *faces, rate, particular, high, low)
    return swept


def solution(mesh):
    placed = (
        P("slab", "modes"),
        P("modes", None, None, None),
        P("modes", None),
        P("modes"),
        P(),
        P("modes"),
        P("modes"),
        P("modes", None, None),
        P(None, "modes"),
        P(None, "modes"),
        P(),
    )

    return jax.shard_map(
        per_device, mesh=mesh, in_specs=placed, out_specs=P("slab", "modes"), check_vma=False
    )
```

```python
import functools

import jax
import jax.numpy as jnp
from jax import lax
from jax.experimental import pallas as pl
from jax.experimental.pallas import tpu as pltpu
from jax.sharding import PartitionSpec as P


BLK = 128
SHELL = 4
SIDE = 4
LAYERS = 8
LATERAL = 16
WIDTH = SHELL * BLK
CELL = LAYERS * LATERAL
HALF = CELL // 2


def route(axis, step):
    pairs = []
    for z in range(SIDE):
        for y in range(SIDE):
            for x in range(SIDE):
                there = [z, y, x]
                there[axis] = (there[axis] + step) % SIDE
                pairs.append(
                    ((z * SIDE + y) * SIDE + x, (there[0] * SIDE + there[1]) * SIDE + there[2])
                )
    return pairs


def send(block, axis, step):
    return lax.ppermute(block, "modes", route(axis, step))


def target(segment, place, i):
    _, _, z_step, upper, pair, step = segment
    along = pair + i
    y, x = (along, step) if upper else (step, along)
    z = ((place >> 4) + z_step) & 3
    return z * 16 + (((place >> 2) + y) & 3) * 4 + ((place + x) & 3)


def partial_kernel(jobs, addends, place_ref, pattern_ref, x_ref, weight_ref, *refs):
    segments = sum(len(job) for job in jobs)
    slopes, couplings = refs[:segments], refs[segments : 2 * segments]
    refs = refs[2 * segments :]
    added, outs = refs[:addends], refs[addends : addends + len(jobs)]
    rounded, warmth = refs[addends + len(jobs) :]
    step = pl.program_id(0)

    @pl.when(step == 0)
    def _():
        prior = x_ref[...]
        rounded[...] = prior.astype(jnp.bfloat16)
        total = jnp.sum(prior * weight_ref[...], axis=1, keepdims=True)
        warmth[...] = jnp.broadcast_to(total, warmth.shape)

    n = 0
    for index, job in enumerate(jobs):
        out_ref = outs[index]
        base = 0
        for segment in job:
            from_row, count = segment[:2]
            cells = pl.ds(from_row, count)
            rows = pl.ds(base, count)
            group = target(segment, place_ref[0], step)
            heat = warmth[cells, :]
            for t in range(SHELL):
                lanes = pl.ds(t * BLK, BLK)
                start = heat * slopes[n][0, :, lanes]
                if addends:
                    start += added[index][0, rows, lanes]
                out_ref[0, rows, lanes] = start
            for b in range(SHELL):
                product = jnp.dot(
                    rounded[cells, pl.ds(b * BLK, BLK)],
                    couplings[n][b, 0],
                    preferred_element_type=jnp.float32,
                )
                where = pattern_ref[b, group]
                lanes = pl.ds(pl.multiple_of(where * BLK, BLK), BLK)
                out_ref[0, rows, lanes] += product
            base += count
            n += 1


def partial_sums(jobs, units, addends, place, pattern, prior, weights, slope, coupling):
    segments = [segment for job in jobs for segment in job]
    slope_specs = [
        pl.BlockSpec(
            (1, 1, WIDTH), functools.partial(lambda n, i, m, p: (target(n, m[0], i), 0, 0), n)
        )
        for n in segments
    ]
    coupling_specs = [
        pl.BlockSpec(
            (SHELL, 1, BLK, BLK),
            functools.partial(lambda n, i, m, p: (0, target(n, m[0], i), 0, 0), n),
        )
        for n in segments
    ]
    heights = [sum(segment[1] for segment in job) for job in jobs]
    blocks = [pl.BlockSpec((1, rows, WIDTH), lambda i, g, p: (i, 0, 0)) for rows in heights]
    return pl.pallas_call(
        functools.partial(partial_kernel, jobs, len(addends)),
        grid_spec=pltpu.PrefetchScalarGridSpec(
            num_scalar_prefetch=2,
            grid=(units,),
            in_specs=[
                pl.BlockSpec((CELL, WIDTH), lambda i, g, p: (0, 0)),
                pl.BlockSpec((1, WIDTH), lambda i, g, p: (0, 0)),
            ]
            + slope_specs
            + coupling_specs
            + blocks[: len(addends)],
            out_specs=blocks,
            scratch_shapes=[
                pltpu.VMEM((CELL, WIDTH), jnp.bfloat16),
                pltpu.VMEM((CELL, BLK), jnp.float32),
            ],
        ),
        out_shape=[jax.ShapeDtypeStruct((units, rows, WIDTH), jnp.float32) for rows in heights],
        cost_estimate=pl.CostEstimate(
            flops=2 * sum(heights) * units * WIDTH * BLK,
            bytes_accessed=sum(heights) * units * WIDTH * 6,
            transcendentals=0,
        ),
        name="partial_sums",
    )(
        place,
        pattern,
        prior,
        weights,
        *([slope] * len(segments)),
        *([coupling] * len(segments)),
        *addends,
    )


def powers_kernel(rate_ref, inscatter_ref, high_ref, low_ref):
    row = lax.broadcasted_iota(jnp.int32, (BLK, BLK), 0)
    column = lax.broadcasted_iota(jnp.int32, (BLK, BLK), 1)
    unit = jnp.where(row == column, 1.0, 0.0).astype(jnp.float32)
    now = [unit + inscatter_ref[b] for b in range(SHELL)]
    for k in range(LAYERS):
        for b in range(SHELL):
            high = now[b].astype(jnp.bfloat16)
            high_ref[b, k] = high
            low_ref[b, k] = (now[b] - high.astype(jnp.float32)).astype(jnp.bfloat16)
            if k + 1 < LAYERS:
                now[b] = product(
                    now[b] * rate_ref[:, pl.ds(b * BLK, BLK)], high_ref[b, 0], low_ref[b, 0]
                )


def product(face, high, low):
    top = face.astype(jnp.bfloat16)
    rest = (face - top.astype(jnp.float32)).astype(jnp.bfloat16)
    rows = face.shape[0]
    both = jnp.dot(
        jnp.concatenate([top, rest], axis=0), high, preferred_element_type=jnp.float32
    )
    return both[:rows] + both[rows:] + jnp.dot(top, low, preferred_element_type=jnp.float32)


def last_kernel(direction_ref, *refs):
    halves, wholes, quarters = refs[:8], refs[8:10], refs[10:12]
    high_ref, low_ref, source_ref, out_ref = refs[12:]
    for side in range(2):
        rows = pl.ds(side * HALF, HALF)
        total = quarters[side][...]
        for part in halves[4 * side : 4 * side + 4]:
            total += part[...]
        for part in wholes:
            total += part[rows, :]
        source_ref[rows, :] = total
    for b in range(SHELL):
        lanes = pl.ds(b * BLK, BLK)
        up = direction_ref[b] == 1
        total = jnp.zeros((LATERAL, BLK), jnp.float32)
        for t in range(LAYERS):
            k = jnp.where(up, LAYERS - 1 - t, t)
            total += product(
                source_ref[pl.ds(t * LATERAL, LATERAL), lanes], high_ref[b, k], low_ref[b, k]
            )
        out_ref[:, lanes] = total


def particular_kernel(direction_ref, source_ref, rate_ref, high_ref, low_ref, out_ref):
    now = [jnp.zeros((LATERAL, BLK), jnp.float32) for _ in range(SHELL)]
    for t in range(LAYERS):
        for b in range(SHELL):
            lanes = pl.ds(b * BLK, BLK)
            at = jnp.where(direction_ref[b] == 1, t, LAYERS - 1 - t)
            rows = pl.ds(pl.multiple_of(at * LATERAL, LATERAL), LATERAL)
            now[b] = product(
                source_ref[rows, lanes] + rate_ref[:, lanes] * now[b], high_ref[b, 0], low_ref[b, 0]
            )
            out_ref[rows, lanes] = now[b]


def finish_kernel(
    direction_ref,
    slab_ref,
    wall_ref,
    one_ref,
    two_ref,
    three_ref,
    rate_ref,
    particular_ref,
    high_ref,
    low_ref,
    out_ref,
    faces,
):
    for k, face in enumerate((one_ref, two_ref, three_ref)):
        faces[k] = face[...]
    slab = slab_ref[0]
    now = [wall_ref[:, pl.ds(b * BLK, BLK)] for b in range(SHELL)]
    for n in range(3):
        for b in range(SHELL):
            lanes = pl.ds(b * BLK, BLK)
            up = direction_ref[b] == 1
            k = jnp.where(up, 2 - n, n)
            active = jnp.where(
                up, (k + 1 <= slab).astype(jnp.int32), (k + 1 > slab).astype(jnp.int32)
            )
            moved = faces[k, :, lanes] + product(
                now[b] * rate_ref[:, lanes], high_ref[b, LAYERS - 1], low_ref[b, LAYERS - 1]
            )
            now[b] = jnp.where(active == 1, moved, now[b])
    for b in range(SHELL):
        lanes = pl.ds(b * BLK, BLK)
        up = direction_ref[b] == 1
        scaled = now[b] * rate_ref[:, lanes]
        for t in range(LAYERS):
            k = jnp.where(up, t, LAYERS - 1 - t)
            rows = pl.ds(t * LATERAL, LATERAL)
            out_ref[rows, lanes] = particular_ref[rows, lanes] + product(
                scaled, high_ref[b, k], low_ref[b, k]
            )


SMEM = pl.BlockSpec(memory_space=pltpu.SMEM)
VMEM = pl.BlockSpec(memory_space=pltpu.VMEM)


def small_call(kernel, outs, specs, scratch=(), flops=0):
    return pl.pallas_call(
        kernel,
        in_specs=specs,
        out_specs=[VMEM] * len(outs),
        out_shape=[jax.ShapeDtypeStruct(*out) for out in outs],
        scratch_shapes=list(scratch),
        cost_estimate=pl.CostEstimate(flops=flops, bytes_accessed=3 << 20, transcendentals=0),
    )


def per_device(
    occupation_prior,
    coupling,
    pattern,
    pseudo_weights,
    equilibrium_slope,
    direction,
    stream_rate,
    inscatter,
    inflow_low,
    inflow_high,
    front_of_row,
):
    modes = lax.axis_index("modes").astype(jnp.int32)
    slab = lax.axis_index("slab").astype(jnp.int32)
    weights = pseudo_weights.reshape(1, WIDTH)
    rate = stream_rate.reshape(1, WIDTH)
    slope = equilibrium_slope.reshape(SIDE**3, 1, WIDTH)
    make = functools.partial(
        partial_sums,
        place=modes.reshape(1),
        pattern=pattern,
        weights=weights,
        slope=slope,
        coupling=coupling,
    )

    def ring_sums(low_step, high_step, prior, addends=()):
        jobs = [
            (
                (0, CELL, 1 if upper else 3, upper, pair, step),
                (0 if upper else HALF, HALF, 2, upper, pair, step),
            )
            for upper in (True, False)
            for pair, step in ((0, low_step), (2, high_step))
        ]
        return make(tuple(jobs), 2, addends, prior=prior)

    def ring(blocks, step):
        axes = (2, 2, 1, 1)
        signs = (step, -step, step, -step)
        moved = []
        for index, block in enumerate(blocks):
            moved.append(send(block, axes[index], signs[index]))
        return moved

    def spread(blocks, axis):
        return [send(block, axis, step) for block, step in zip(blocks, (1, 2, -1))]

    prior = occupation_prior
    split = [((SHELL, LAYERS, BLK, BLK), jnp.bfloat16)] * 2
    high, low = small_call(powers_kernel, split, [VMEM, VMEM], flops=200_000_000)(rate, inscatter)
    picks = front_of_row[:, None] == jnp.arange(inflow_low.shape[0], dtype=jnp.int32)[None, :]
    ahead = (jnp.repeat(direction, BLK) == 1)[None, :]
    inflow = jnp.where(ahead, inflow_low, inflow_high)
    wall = jnp.sum(jnp.where(picks[:, :, None], inflow[None, :, :], 0.0), axis=1)

    far_got = ring(ring_sums(2, 2, prior), 1)
    direct = ring_sums(3, 1, prior)
    early = ring(direct, -1)
    after, _ = lax.optimization_barrier((prior, direct))
    near = make(
        tuple(
            ((0 if upper else HALF, HALF, 0, upper, 0, step),)
            for upper in (True, False)
            for step in range(SIDE)
        ),
        SIDE,
        (),
        prior=after,
    )
    far_got, near = lax.optimization_barrier((far_got, near))
    beside = ((near[1], 2, 1), (near[3], 2, -1), (near[5], 1, 1), (near[7], 1, -1))
    late = ring(ring_sums(1, 3, prior, far_got), 1)
    early, high, low, wall = lax.optimization_barrier((early, high, low, wall))
    kept = ring_sums(0, 0, prior, early)
    a1, a3, a2 = kept[0][1] + late[0][1], kept[1][1] + late[1][1], kept[1][0] + late[1][0]
    b1, b3, b2 = kept[2][1] + late[2][1], kept[3][1] + late[3][1], kept[3][0] + late[3][0]
    near_got = []
    for block, axis, step in beside:
        near_got.append(send(block, axis, step))
    a_got = spread((a1, a2, a3), 1)
    b_got = spread((b1, b2, b3), 2)
    a_own, a_got = lax.optimization_barrier(((kept[0], late[0]), a_got))
    b_own, b_got = lax.optimization_barrier(((kept[2], late[2]), b_got))
    a_sum = a_own[0][0] + a_own[1][0] + a_got[0] + a_got[1] + a_got[2]
    b_sum = b_own[0][0] + b_own[1][0] + b_got[0] + b_got[1] + b_got[2]
    depth = []
    for block, step in ((a_sum[:CELL], 1), (a_sum[CELL:], 2), (b_sum[:CELL], -1), (b_sum[CELL:], 2)):
        depth.append(send(block, 0, step))
    from_below, far_a, from_above, far_b = depth
    across, _ = lax.optimization_barrier(((near[2], near[6]), (a_sum, b_sum)))
    far_x = send(across[0], 2, 2)
    far_y = send(across[1], 1, 2)
    near_a = [near_got[0], near_got[1], far_x]
    near_b = [near_got[2], near_got[3], far_y]

    def ends(own, got, axis):
        parts = [own[i] + got[0][i] + got[1][i] + got[2][i] for i in range(SIDE)]
        return [parts[0]] + spread(parts[1:], axis)

    halves = ends(near[0], near_a, 1) + ends(near[4], near_b, 2)

    whole = ((CELL, WIDTH), jnp.float32)
    source, last = small_call(
        last_kernel,
        [whole, ((LATERAL, WIDTH), jnp.float32)],
        [SMEM] + [VMEM] * 14,
        flops=40_000_000,
    )(direction, *halves, from_below, from_above, far_a, far_b, high, low)
    faces = [
        lax.ppermute(last, "slab", [(i, (i + k) % 4) for i in range(4)]) for k in (1, 2, 3)
    ]
    (particular,) = small_call(
        particular_kernel, [whole], [SMEM] + [VMEM] * 4, flops=40_000_000
    )(direction, source, rate, high, low)
    (swept,) = small_call(
        finish_kernel,
        [whole],
        [SMEM, SMEM] + [VMEM] * 8,
        scratch=[pltpu.VMEM((3, LATERAL, WIDTH), jnp.float32)],
        flops=60_000_000,
    )(direction, slab.reshape(1), wall, *faces, rate, particular, high, low)
    return swept


def solution(mesh):
    placed = (
        P("slab", "modes"),
        P("modes", None, None, None),
        P("modes", None),
        P("modes"),
        P(),
        P("modes"),
        P("modes"),
        P("modes", None, None),
        P(None, "modes"),
        P(None, "modes"),
        P(),
    )

    return jax.shard_map(
        per_device, mesh=mesh, in_specs=placed, out_specs=P("slab", "modes"), check_vma=False
    )
```

```python
import functools

import jax
import jax.numpy as jnp
from jax import lax
from jax.experimental import pallas as pl
from jax.experimental.pallas import tpu as pltpu
from jax.sharding import PartitionSpec as P


BLK = 128
SHELL = 4
SIDE = 4
LAYERS = 8
LATERAL = 16
WIDTH = SHELL * BLK
CELL = LAYERS * LATERAL
HALF = CELL // 2


def route(axis, step):
    pairs = []
    for z in range(SIDE):
        for y in range(SIDE):
            for x in range(SIDE):
                there = [z, y, x]
                there[axis] = (there[axis] + step) % SIDE
                pairs.append(
                    ((z * SIDE + y) * SIDE + x, (there[0] * SIDE + there[1]) * SIDE + there[2])
                )
    return pairs


def send(block, axis, step):
    return lax.ppermute(block, "modes", route(axis, step))


def target(segment, place, i):
    _, _, z_step, upper, pair, step = segment
    along = pair + i
    y, x = (along, step) if upper else (step, along)
    z = ((place >> 4) + z_step) & 3
    return z * 16 + (((place >> 2) + y) & 3) * 4 + ((place + x) & 3)


def partial_kernel(jobs, addends, place_ref, pattern_ref, x_ref, weight_ref, *refs):
    segments = sum(len(job) for job in jobs)
    slopes, couplings = refs[:segments], refs[segments : 2 * segments]
    refs = refs[2 * segments :]
    added, outs = refs[:addends], refs[addends : addends + len(jobs)]
    rounded, warmth = refs[addends + len(jobs) :]
    step = pl.program_id(0)

    @pl.when(step == 0)
    def _():
        prior = x_ref[...]
        rounded[...] = prior.astype(jnp.bfloat16)
        total = jnp.sum(prior * weight_ref[...], axis=1, keepdims=True)
        warmth[...] = jnp.broadcast_to(total, warmth.shape)

    n = 0
    for index, job in enumerate(jobs):
        out_ref = outs[index]
        base = 0
        for segment in job:
            from_row, count = segment[:2]
            cells = pl.ds(from_row, count)
            rows = pl.ds(base, count)
            group = target(segment, place_ref[0], step)
            heat = warmth[cells, :]
            for t in range(SHELL):
                lanes = pl.ds(t * BLK, BLK)
                start = heat * slopes[n][0, :, lanes]
                if addends:
                    start += added[index][0, rows, lanes]
                out_ref[0, rows, lanes] = start
            for b in range(SHELL):
                product = jnp.dot(
                    rounded[cells, pl.ds(b * BLK, BLK)],
                    couplings[n][b, 0],
                    preferred_element_type=jnp.float32,
                )
                where = pattern_ref[b, group]
                lanes = pl.ds(pl.multiple_of(where * BLK, BLK), BLK)
                out_ref[0, rows, lanes] += product
            base += count
            n += 1


def partial_sums(jobs, units, addends, place, pattern, prior, weights, slope, coupling):
    segments = [segment for job in jobs for segment in job]
    slope_specs = [
        pl.BlockSpec(
            (1, 1, WIDTH), functools.partial(lambda n, i, m, p: (target(n, m[0], i), 0, 0), n)
        )
        for n in segments
    ]
    coupling_specs = [
        pl.BlockSpec(
            (SHELL, 1, BLK, BLK),
            functools.partial(lambda n, i, m, p: (0, target(n, m[0], i), 0, 0), n),
        )
        for n in segments
    ]
    heights = [sum(segment[1] for segment in job) for job in jobs]
    blocks = [pl.BlockSpec((1, rows, WIDTH), lambda i, g, p: (i, 0, 0)) for rows in heights]
    return pl.pallas_call(
        functools.partial(partial_kernel, jobs, len(addends)),
        grid_spec=pltpu.PrefetchScalarGridSpec(
            num_scalar_prefetch=2,
            grid=(units,),
            in_specs=[
                pl.BlockSpec((CELL, WIDTH), lambda i, g, p: (0, 0)),
                pl.BlockSpec((1, WIDTH), lambda i, g, p: (0, 0)),
            ]
            + slope_specs
            + coupling_specs
            + blocks[: len(addends)],
            out_specs=blocks,
            scratch_shapes=[
                pltpu.VMEM((CELL, WIDTH), jnp.bfloat16),
                pltpu.VMEM((CELL, BLK), jnp.float32),
            ],
        ),
        out_shape=[jax.ShapeDtypeStruct((units, rows, WIDTH), jnp.float32) for rows in heights],
        cost_estimate=pl.CostEstimate(
            flops=2 * sum(heights) * units * WIDTH * BLK,
            bytes_accessed=sum(heights) * units * WIDTH * 6,
            transcendentals=0,
        ),
        name="partial_sums",
    )(
        place,
        pattern,
        prior,
        weights,
        *([slope] * len(segments)),
        *([coupling] * len(segments)),
        *addends,
    )


def powers_kernel(rate_ref, inscatter_ref, high_ref, low_ref):
    row = lax.broadcasted_iota(jnp.int32, (BLK, BLK), 0)
    column = lax.broadcasted_iota(jnp.int32, (BLK, BLK), 1)
    unit = jnp.where(row == column, 1.0, 0.0).astype(jnp.float32)
    now = [unit + inscatter_ref[b] for b in range(SHELL)]
    for k in range(LAYERS):
        for b in range(SHELL):
            high = now[b].astype(jnp.bfloat16)
            high_ref[b, k] = high
            low_ref[b, k] = (now[b] - high.astype(jnp.float32)).astype(jnp.bfloat16)
            if k + 1 < LAYERS:
                now[b] = product(
                    now[b] * rate_ref[:, pl.ds(b * BLK, BLK)], high_ref[b, 0], low_ref[b, 0]
                )


def product(face, high, low):
    top = face.astype(jnp.bfloat16)
    rest = (face - top.astype(jnp.float32)).astype(jnp.bfloat16)
    rows = face.shape[0]
    both = jnp.dot(
        jnp.concatenate([top, rest], axis=0), high, preferred_element_type=jnp.float32
    )
    return both[:rows] + both[rows:] + jnp.dot(top, low, preferred_element_type=jnp.float32)


def last_kernel(direction_ref, *refs):
    halves, wholes, quarters = refs[:8], refs[8:10], refs[10:12]
    high_ref, low_ref, source_ref, out_ref = refs[12:]
    for side in range(2):
        rows = pl.ds(side * HALF, HALF)
        total = quarters[side][...]
        for part in halves[4 * side : 4 * side + 4]:
            total += part[...]
        for part in wholes:
            total += part[rows, :]
        source_ref[rows, :] = total
    for b in range(SHELL):
        lanes = pl.ds(b * BLK, BLK)
        up = direction_ref[b] == 1
        total = jnp.zeros((LATERAL, BLK), jnp.float32)
        for t in range(LAYERS):
            k = jnp.where(up, LAYERS - 1 - t, t)
            total += product(
                source_ref[pl.ds(t * LATERAL, LATERAL), lanes], high_ref[b, k], low_ref[b, k]
            )
        out_ref[:, lanes] = total


def particular_kernel(direction_ref, source_ref, rate_ref, high_ref, low_ref, out_ref):
    now = [jnp.zeros((LATERAL, BLK), jnp.float32) for _ in range(SHELL)]
    for t in range(LAYERS):
        for b in range(SHELL):
            lanes = pl.ds(b * BLK, BLK)
            at = jnp.where(direction_ref[b] == 1, t, LAYERS - 1 - t)
            rows = pl.ds(pl.multiple_of(at * LATERAL, LATERAL), LATERAL)
            now[b] = product(
                source_ref[rows, lanes] + rate_ref[:, lanes] * now[b], high_ref[b, 0], low_ref[b, 0]
            )
            out_ref[rows, lanes] = now[b]


def finish_kernel(
    direction_ref,
    slab_ref,
    wall_ref,
    one_ref,
    two_ref,
    three_ref,
    rate_ref,
    particular_ref,
    high_ref,
    low_ref,
    out_ref,
    faces,
):
    for k, face in enumerate((one_ref, two_ref, three_ref)):
        faces[k] = face[...]
    slab = slab_ref[0]
    now = [wall_ref[:, pl.ds(b * BLK, BLK)] for b in range(SHELL)]
    for n in range(3):
        for b in range(SHELL):
            lanes = pl.ds(b * BLK, BLK)
            up = direction_ref[b] == 1
            k = jnp.where(up, 2 - n, n)
            active = jnp.where(
                up, (k + 1 <= slab).astype(jnp.int32), (k + 1 > slab).astype(jnp.int32)
            )
            moved = faces[k, :, lanes] + product(
                now[b] * rate_ref[:, lanes], high_ref[b, LAYERS - 1], low_ref[b, LAYERS - 1]
            )
            now[b] = jnp.where(active == 1, moved, now[b])
    for b in range(SHELL):
        lanes = pl.ds(b * BLK, BLK)
        up = direction_ref[b] == 1
        scaled = now[b] * rate_ref[:, lanes]
        for t in range(LAYERS):
            k = jnp.where(up, t, LAYERS - 1 - t)
            rows = pl.ds(t * LATERAL, LATERAL)
            out_ref[rows, lanes] = particular_ref[rows, lanes] + product(
                scaled, high_ref[b, k], low_ref[b, k]
            )


SMEM = pl.BlockSpec(memory_space=pltpu.SMEM)
VMEM = pl.BlockSpec(memory_space=pltpu.VMEM)


def small_call(kernel, outs, specs, scratch=(), flops=0):
    return pl.pallas_call(
        kernel,
        in_specs=specs,
        out_specs=[VMEM] * len(outs),
        out_shape=[jax.ShapeDtypeStruct(*out) for out in outs],
        scratch_shapes=list(scratch),
        cost_estimate=pl.CostEstimate(flops=flops, bytes_accessed=3 << 20, transcendentals=0),
    )


def per_device(
    occupation_prior,
    coupling,
    pattern,
    pseudo_weights,
    equilibrium_slope,
    direction,
    stream_rate,
    inscatter,
    inflow_low,
    inflow_high,
    front_of_row,
):
    modes = lax.axis_index("modes").astype(jnp.int32)
    slab = lax.axis_index("slab").astype(jnp.int32)
    weights = pseudo_weights.reshape(1, WIDTH)
    rate = stream_rate.reshape(1, WIDTH)
    slope = equilibrium_slope.reshape(SIDE**3, 1, WIDTH)
    make = functools.partial(
        partial_sums,
        place=modes.reshape(1),
        pattern=pattern,
        weights=weights,
        slope=slope,
        coupling=coupling,
    )

    def ring_sums(low_step, high_step, prior, addends=()):
        jobs = [
            (
                (0, CELL, 1 if upper else 3, upper, pair, step),
                (0 if upper else HALF, HALF, 2, upper, pair, step),
            )
            for upper in (True, False)
            for pair, step in ((0, low_step), (2, high_step))
        ]
        return make(tuple(jobs), 2, addends, prior=prior)

    def ring(blocks, step):
        axes = (2, 2, 1, 1)
        signs = (step, -step, step, -step)
        moved = []
        for index, block in enumerate(blocks):
            moved.append(send(block, axes[index], signs[index]))
        return moved

    def spread(blocks, axis):
        return [send(block, axis, step) for block, step in zip(blocks, (1, 2, -1))]

    prior = occupation_prior
    split = [((SHELL, LAYERS, BLK, BLK), jnp.bfloat16)] * 2
    high, low = small_call(powers_kernel, split, [VMEM, VMEM], flops=200_000_000)(rate, inscatter)
    picks = front_of_row[:, None] == jnp.arange(inflow_low.shape[0], dtype=jnp.int32)[None, :]
    ahead = (jnp.repeat(direction, BLK) == 1)[None, :]
    inflow = jnp.where(ahead, inflow_low, inflow_high)
    wall = jnp.sum(jnp.where(picks[:, :, None], inflow[None, :, :], 0.0), axis=1)

    far_got = ring(ring_sums(2, 2, prior), 1)
    direct = ring_sums(3, 1, prior)
    early = ring(direct, -1)
    after, _ = lax.optimization_barrier((prior, direct))
    near = make(
        tuple(
            ((0 if upper else HALF, HALF, 0, upper, 0, step),)
            for upper in (True, False)
            for step in range(SIDE)
        ),
        SIDE,
        (),
        prior=after,
    )
    far_got, near = lax.optimization_barrier((far_got, near))
    beside = ((near[1], 2, 1), (near[3], 2, -1), (near[5], 1, 1), (near[7], 1, -1))
    late = ring(ring_sums(1, 3, prior, far_got), 1)
    early, high, low, wall = lax.optimization_barrier((early, high, low, wall))
    kept = ring_sums(0, 0, prior, early)
    a1, a3, a2 = kept[0][1] + late[0][1], kept[1][1] + late[1][1], kept[1][0] + late[1][0]
    b1, b3, b2 = kept[2][1] + late[2][1], kept[3][1] + late[3][1], kept[3][0] + late[3][0]
    near_got = []
    for block, axis, step in beside:
        near_got.append(send(block, axis, step))
    crossed = []
    for block, axis, step in ((a1, 1, 1), (a2, 1, 2), (a3, 1, -1), (b1, 2, 1), (b2, 2, 2), (b3, 2, -1)):
        crossed.append(send(block, axis, step))
    a_got, b_got = crossed[:3], crossed[3:]
    ready_a = near[0] + near_got[0] + near_got[1]
    ready_b = near[4] + near_got[2] + near_got[3]
    ready_a, ready_b = lax.optimization_barrier((ready_a, ready_b))
    across, _ = lax.optimization_barrier(((near[2], near[6]), (a_got, b_got)))
    far_x = send(across[0], 2, 2)
    far_y = send(across[1], 1, 2)
    a_own, a_got = lax.optimization_barrier(((kept[0], late[0]), a_got))
    b_own, b_got = lax.optimization_barrier(((kept[2], late[2]), b_got))
    a_sum = a_own[0][0] + a_own[1][0] + a_got[0] + a_got[1] + a_got[2]
    b_sum = b_own[0][0] + b_own[1][0] + b_got[0] + b_got[1] + b_got[2]
    depth = []
    for block, step in ((a_sum[:CELL], 1), (b_sum[:CELL], -1), (a_sum[CELL:], 2), (b_sum[CELL:], 2)):
        depth.append(send(block, 0, step))
    from_below, from_above, far_a, far_b = depth

    def ends(ready, got, axis):
        parts = [ready[i] + got[i] for i in range(SIDE)]
        return [parts[0]] + spread(parts[1:], axis)

    halves = ends(ready_a, far_x, 1) + ends(ready_b, far_y, 2)

    whole = ((CELL, WIDTH), jnp.float32)
    source, last = small_call(
        last_kernel,
        [whole, ((LATERAL, WIDTH), jnp.float32)],
        [SMEM] + [VMEM] * 14,
        flops=40_000_000,
    )(direction, *halves, from_below, from_above, far_a, far_b, high, low)
    faces = [
        lax.ppermute(last, "slab", [(i, (i + k) % 4) for i in range(4)]) for k in (1, 2, 3)
    ]
    (particular,) = small_call(
        particular_kernel, [whole], [SMEM] + [VMEM] * 4, flops=40_000_000
    )(direction, source, rate, high, low)
    (swept,) = small_call(
        finish_kernel,
        [whole],
        [SMEM, SMEM] + [VMEM] * 8,
        scratch=[pltpu.VMEM((3, LATERAL, WIDTH), jnp.float32)],
        flops=60_000_000,
    )(direction, slab.reshape(1), wall, *faces, rate, particular, high, low)
    return swept


def solution(mesh):
    placed = (
        P("slab", "modes"),
        P("modes", None, None, None),
        P("modes", None),
        P("modes"),
        P(),
        P("modes"),
        P("modes"),
        P("modes", None, None),
        P(None, "modes"),
        P(None, "modes"),
        P(),
    )

    return jax.shard_map(
        per_device, mesh=mesh, in_specs=placed, out_specs=P("slab", "modes"), check_vma=False
    )
```

```python
import functools

import jax
import jax.numpy as jnp
from jax import lax
from jax.experimental import pallas as pl
from jax.experimental.pallas import tpu as pltpu
from jax.sharding import PartitionSpec as P


BLK = 128
SHELL = 4
SIDE = 4
LAYERS = 8
LATERAL = 16
WIDTH = SHELL * BLK
CELL = LAYERS * LATERAL
HALF = CELL // 2


def route(axis, step):
    pairs = []
    for z in range(SIDE):
        for y in range(SIDE):
            for x in range(SIDE):
                there = [z, y, x]
                there[axis] = (there[axis] + step) % SIDE
                pairs.append(
                    ((z * SIDE + y) * SIDE + x, (there[0] * SIDE + there[1]) * SIDE + there[2])
                )
    return pairs


def send(block, axis, step):
    return lax.ppermute(block, "modes", route(axis, step))


def target(segment, place, i):
    _, _, z_step, upper, pair, step = segment
    along = pair + i
    y, x = (along, step) if upper else (step, along)
    z = ((place >> 4) + z_step) & 3
    return z * 16 + (((place >> 2) + y) & 3) * 4 + ((place + x) & 3)


def partial_kernel(jobs, addends, place_ref, pattern_ref, x_ref, weight_ref, *refs):
    segments = sum(len(job) for job in jobs)
    slopes, couplings = refs[:segments], refs[segments : 2 * segments]
    refs = refs[2 * segments :]
    added, outs = refs[:addends], refs[addends : addends + len(jobs)]
    rounded, warmth = refs[addends + len(jobs) :]
    step = pl.program_id(0)

    @pl.when(step == 0)
    def _():
        prior = x_ref[...]
        rounded[...] = prior.astype(jnp.bfloat16)
        total = jnp.sum(prior * weight_ref[...], axis=1, keepdims=True)
        warmth[...] = jnp.broadcast_to(total, warmth.shape)

    n = 0
    for index, job in enumerate(jobs):
        out_ref = outs[index]
        base = 0
        for segment in job:
            from_row, count = segment[:2]
            cells = pl.ds(from_row, count)
            rows = pl.ds(base, count)
            group = target(segment, place_ref[0], step)
            heat = warmth[cells, :]
            for t in range(SHELL):
                lanes = pl.ds(t * BLK, BLK)
                start = heat * slopes[n][0, :, lanes]
                if addends:
                    start += added[index][0, rows, lanes]
                out_ref[0, rows, lanes] = start
            for b in range(SHELL):
                product = jnp.dot(
                    rounded[cells, pl.ds(b * BLK, BLK)],
                    couplings[n][b, 0],
                    preferred_element_type=jnp.float32,
                )
                where = pattern_ref[b, group]
                lanes = pl.ds(pl.multiple_of(where * BLK, BLK), BLK)
                out_ref[0, rows, lanes] += product
            base += count
            n += 1


def partial_sums(jobs, units, addends, place, pattern, prior, weights, slope, coupling):
    segments = [segment for job in jobs for segment in job]
    slope_specs = [
        pl.BlockSpec(
            (1, 1, WIDTH), functools.partial(lambda n, i, m, p: (target(n, m[0], i), 0, 0), n)
        )
        for n in segments
    ]
    coupling_specs = [
        pl.BlockSpec(
            (SHELL, 1, BLK, BLK),
            functools.partial(lambda n, i, m, p: (0, target(n, m[0], i), 0, 0), n),
        )
        for n in segments
    ]
    heights = [sum(segment[1] for segment in job) for job in jobs]
    blocks = [pl.BlockSpec((1, rows, WIDTH), lambda i, g, p: (i, 0, 0)) for rows in heights]
    return pl.pallas_call(
        functools.partial(partial_kernel, jobs, len(addends)),
        grid_spec=pltpu.PrefetchScalarGridSpec(
            num_scalar_prefetch=2,
            grid=(units,),
            in_specs=[
                pl.BlockSpec((CELL, WIDTH), lambda i, g, p: (0, 0)),
                pl.BlockSpec((1, WIDTH), lambda i, g, p: (0, 0)),
            ]
            + slope_specs
            + coupling_specs
            + blocks[: len(addends)],
            out_specs=blocks,
            scratch_shapes=[
                pltpu.VMEM((CELL, WIDTH), jnp.bfloat16),
                pltpu.VMEM((CELL, BLK), jnp.float32),
            ],
        ),
        out_shape=[jax.ShapeDtypeStruct((units, rows, WIDTH), jnp.float32) for rows in heights],
        cost_estimate=pl.CostEstimate(
            flops=2 * sum(heights) * units * WIDTH * BLK,
            bytes_accessed=sum(heights) * units * WIDTH * 6,
            transcendentals=0,
        ),
        name="partial_sums",
    )(
        place,
        pattern,
        prior,
        weights,
        *([slope] * len(segments)),
        *([coupling] * len(segments)),
        *addends,
    )


def powers_kernel(rate_ref, inscatter_ref, high_ref, low_ref):
    row = lax.broadcasted_iota(jnp.int32, (BLK, BLK), 0)
    column = lax.broadcasted_iota(jnp.int32, (BLK, BLK), 1)
    unit = jnp.where(row == column, 1.0, 0.0).astype(jnp.float32)

    def raise_power(k, now):
        raised = []
        for b in range(SHELL):
            high = now[b].astype(jnp.bfloat16)
            high_ref[b, k] = high
            low_ref[b, k] = (now[b] - high.astype(jnp.float32)).astype(jnp.bfloat16)
            raised.append(
                product(now[b] * rate_ref[:, pl.ds(b * BLK, BLK)], high_ref[b, 0], low_ref[b, 0])
            )
        return tuple(raised)

    lax.fori_loop(0, LAYERS, raise_power, tuple(unit + inscatter_ref[b] for b in range(SHELL)))


def product(face, high, low):
    top = face.astype(jnp.bfloat16)
    rest = (face - top.astype(jnp.float32)).astype(jnp.bfloat16)
    rows = face.shape[0]
    both = jnp.dot(
        jnp.concatenate([top, rest], axis=0), high, preferred_element_type=jnp.float32
    )
    return both[:rows] + both[rows:] + jnp.dot(top, low, preferred_element_type=jnp.float32)


def last_kernel(direction_ref, *refs):
    halves, wholes = refs[:8], refs[8:10]
    high_ref, low_ref, source_ref, out_ref = refs[10:]
    for side in range(2):
        rows = pl.ds(side * HALF, HALF)
        total = halves[4 * side][...]
        for part in halves[4 * side + 1 : 4 * side + 4]:
            total += part[...]
        for part in wholes:
            total += part[rows, :]
        source_ref[rows, :] = total
    for b in range(SHELL):
        lanes = pl.ds(b * BLK, BLK)
        up = direction_ref[b] == 1
        total = jnp.zeros((LATERAL, BLK), jnp.float32)
        for t in range(LAYERS):
            k = jnp.where(up, LAYERS - 1 - t, t)
            total += product(
                source_ref[pl.ds(t * LATERAL, LATERAL), lanes], high_ref[b, k], low_ref[b, k]
            )
        out_ref[:, lanes] = total


def particular_kernel(direction_ref, source_ref, rate_ref, high_ref, low_ref, out_ref):
    now = [jnp.zeros((LATERAL, BLK), jnp.float32) for _ in range(SHELL)]
    for t in range(LAYERS):
        for b in range(SHELL):
            lanes = pl.ds(b * BLK, BLK)
            at = jnp.where(direction_ref[b] == 1, t, LAYERS - 1 - t)
            rows = pl.ds(pl.multiple_of(at * LATERAL, LATERAL), LATERAL)
            now[b] = product(
                source_ref[rows, lanes] + rate_ref[:, lanes] * now[b], high_ref[b, 0], low_ref[b, 0]
            )
            out_ref[rows, lanes] = now[b]


def finish_kernel(
    direction_ref,
    slab_ref,
    wall_ref,
    one_ref,
    two_ref,
    three_ref,
    rate_ref,
    particular_ref,
    high_ref,
    low_ref,
    out_ref,
    faces,
):
    for k, face in enumerate((one_ref, two_ref, three_ref)):
        faces[k] = face[...]
    slab = slab_ref[0]
    now = [wall_ref[:, pl.ds(b * BLK, BLK)] for b in range(SHELL)]
    for n in range(3):
        for b in range(SHELL):
            lanes = pl.ds(b * BLK, BLK)
            up = direction_ref[b] == 1
            k = jnp.where(up, 2 - n, n)
            active = jnp.where(
                up, (k + 1 <= slab).astype(jnp.int32), (k + 1 > slab).astype(jnp.int32)
            )
            moved = faces[k, :, lanes] + product(
                now[b] * rate_ref[:, lanes], high_ref[b, LAYERS - 1], low_ref[b, LAYERS - 1]
            )
            now[b] = jnp.where(active == 1, moved, now[b])
    for b in range(SHELL):
        lanes = pl.ds(b * BLK, BLK)
        up = direction_ref[b] == 1
        scaled = now[b] * rate_ref[:, lanes]
        for t in range(LAYERS):
            k = jnp.where(up, t, LAYERS - 1 - t)
            rows = pl.ds(t * LATERAL, LATERAL)
            out_ref[rows, lanes] = particular_ref[rows, lanes] + product(
                scaled, high_ref[b, k], low_ref[b, k]
            )


SMEM = pl.BlockSpec(memory_space=pltpu.SMEM)
VMEM = pl.BlockSpec(memory_space=pltpu.VMEM)


FIRST = pl.BlockSpec((SHELL, 1, BLK, BLK), lambda i: (0, 0, 0, 0))


def small_call(kernel, outs, specs, scratch=(), flops=0, grid=()):
    return pl.pallas_call(
        kernel,
        grid=grid,
        in_specs=specs,
        out_specs=[VMEM] * len(outs),
        out_shape=[jax.ShapeDtypeStruct(*out) for out in outs],
        scratch_shapes=list(scratch),
        cost_estimate=pl.CostEstimate(flops=flops, bytes_accessed=3 << 20, transcendentals=0),
    )


def per_device(
    occupation_prior,
    coupling,
    pattern,
    pseudo_weights,
    equilibrium_slope,
    direction,
    stream_rate,
    inscatter,
    inflow_low,
    inflow_high,
    front_of_row,
):
    modes = lax.axis_index("modes").astype(jnp.int32)
    slab = lax.axis_index("slab").astype(jnp.int32)
    weights = pseudo_weights.reshape(1, WIDTH)
    rate = stream_rate.reshape(1, WIDTH)
    slope = equilibrium_slope.reshape(SIDE**3, 1, WIDTH)
    make = functools.partial(
        partial_sums,
        place=modes.reshape(1),
        pattern=pattern,
        weights=weights,
        slope=slope,
        coupling=coupling,
    )

    def ring_sums(low_step, high_step, prior, addends=()):
        jobs = [
            (
                (0, CELL, 1 if upper else 3, upper, pair, step),
                (0 if upper else HALF, HALF, 2, upper, pair, step),
            )
            for upper in (True, False)
            for pair, step in ((0, low_step), (2, high_step))
        ]
        return make(tuple(jobs), 2, addends, prior=prior)

    def ring(blocks, step):
        axes = (2, 2, 1, 1)
        signs = (step, -step, step, -step)
        moved = []
        for index, block in enumerate(blocks):
            moved.append(send(block, axes[index], signs[index]))
        return moved

    prior = occupation_prior
    split = [((SHELL, LAYERS, BLK, BLK), jnp.bfloat16)] * 2
    high, low = small_call(powers_kernel, split, [VMEM, VMEM], flops=200_000_000)(rate, inscatter)
    picks = front_of_row[:, None] == jnp.arange(inflow_low.shape[0], dtype=jnp.int32)[None, :]
    ahead = (jnp.repeat(direction, BLK) == 1)[None, :]
    inflow = jnp.where(ahead, inflow_low, inflow_high)
    wall = jnp.sum(jnp.where(picks[:, :, None], inflow[None, :, :], 0.0), axis=1)

    far_got = ring(ring_sums(2, 2, prior), 1)
    direct = ring_sums(3, 1, prior)
    early = ring(direct, -1)
    after, _ = lax.optimization_barrier((prior, direct))
    near = make(
        tuple(
            ((0 if upper else HALF, HALF, 0, upper, 0, step),)
            for upper in (True, False)
            for step in range(SIDE)
        ),
        SIDE,
        (),
        prior=after,
    )
    far_got, near = lax.optimization_barrier((far_got, near))
    beside = ((near[1], 2, 1), (near[3], 2, -1), (near[5], 1, 1), (near[7], 1, -1))
    late = ring(ring_sums(1, 3, prior, far_got), 1)
    early, high, low, wall = lax.optimization_barrier((early, high, low, wall))
    kept = ring_sums(0, 0, prior, early)
    a1, a3, a2 = kept[0][1] + late[0][1], kept[1][1] + late[1][1], kept[1][0] + late[1][0]
    b1, b3, b2 = kept[2][1] + late[2][1], kept[3][1] + late[3][1], kept[3][0] + late[3][0]
    near_got = []
    for block, axis, step in beside:
        near_got.append(send(block, axis, step))
    crossed = []
    for block, axis, step in ((a1, 1, 1), (a2, 1, 2), (a3, 1, -1), (b1, 2, 1), (b2, 2, 2), (b3, 2, -1)):
        crossed.append(send(block, axis, step))
    a_got, b_got = crossed[:3], crossed[3:]
    ready_a = near[0] + near_got[0] + near_got[1]
    ready_b = near[4] + near_got[2] + near_got[3]
    ready_a, ready_b = lax.optimization_barrier((ready_a, ready_b))
    across, _ = lax.optimization_barrier(((near[2], near[6]), (a_got, b_got)))
    far_x = send(across[0], 2, 2)
    far_y = send(across[1], 1, 2)
    a_own, a_got = lax.optimization_barrier(((kept[0], late[0]), a_got))
    b_own, b_got = lax.optimization_barrier(((kept[2], late[2]), b_got))
    a_sum = a_own[0][0] + a_own[1][0] + a_got[0] + a_got[1] + a_got[2]
    b_sum = b_own[0][0] + b_own[1][0] + b_got[0] + b_got[1] + b_got[2]
    far_up = send(a_sum[CELL:], 0, 1)
    far_down = send(b_sum[CELL:], 0, -1)
    above = jnp.concatenate([a_sum[:HALF] + far_up, a_sum[HALF:CELL]], axis=0)
    below = jnp.concatenate([b_sum[:HALF], b_sum[HALF:CELL] + far_down], axis=0)
    from_below = send(above, 0, 1)
    from_above = send(below, 0, -1)

    def ends(ready, got, axis):
        parts = [ready[i] + got[i] for i in range(SIDE)]
        moved = []
        for index, step in enumerate((1, 2, -1)):
            moved.append(send(parts[index + 1], axis, step))
        return [parts[0]] + moved

    halves = ends(ready_a, far_x, 1) + ends(ready_b, far_y, 2)

    whole = ((CELL, WIDTH), jnp.float32)
    source, last = small_call(
        last_kernel,
        [whole, ((LATERAL, WIDTH), jnp.float32)],
        [SMEM] + [VMEM] * 12,
        flops=40_000_000,
    )(direction, *halves, from_below, from_above, high, low)
    faces = [
        lax.ppermute(last, "slab", [(i, (i + k) % 4) for i in range(4)]) for k in (1, 2, 3)
    ]
    (particular,) = small_call(
        particular_kernel, [whole], [SMEM, VMEM, VMEM, FIRST, FIRST], flops=40_000_000, grid=(1,)
    )(direction, source, rate, high, low)
    (swept,) = small_call(
        finish_kernel,
        [whole],
        [SMEM, SMEM] + [VMEM] * 8,
        scratch=[pltpu.VMEM((3, LATERAL, WIDTH), jnp.float32)],
        flops=60_000_000,
    )(direction, slab.reshape(1), wall, *faces, rate, particular, high, low)
    return swept


def solution(mesh):
    placed = (
        P("slab", "modes"),
        P("modes", None, None, None),
        P("modes", None),
        P("modes"),
        P(),
        P("modes"),
        P("modes"),
        P("modes", None, None),
        P(None, "modes"),
        P(None, "modes"),
        P(),
    )

    return jax.shard_map(
        per_device, mesh=mesh, in_specs=placed, out_specs=P("slab", "modes"), check_vma=False
    )
```

```python
import functools

import jax
import jax.numpy as jnp
from jax import lax
from jax.experimental import pallas as pl
from jax.experimental.pallas import tpu as pltpu
from jax.sharding import PartitionSpec as P


BLK = 128
SHELL = 4
SIDE = 4
LAYERS = 8
LATERAL = 16
WIDTH = SHELL * BLK
CELL = LAYERS * LATERAL
HALF = CELL // 2


def route(axis, step):
    pairs = []
    for z in range(SIDE):
        for y in range(SIDE):
            for x in range(SIDE):
                there = [z, y, x]
                there[axis] = (there[axis] + step) % SIDE
                pairs.append(
                    ((z * SIDE + y) * SIDE + x, (there[0] * SIDE + there[1]) * SIDE + there[2])
                )
    return pairs


def send(block, axis, step):
    return lax.ppermute(block, "modes", route(axis, step))


def target(segment, place, i):
    _, _, z_step, upper, pair, step = segment
    along = pair + i
    y, x = (along, step) if upper else (step, along)
    z = ((place >> 4) + z_step) & 3
    return z * 16 + (((place >> 2) + y) & 3) * 4 + ((place + x) & 3)


def partial_kernel(jobs, addends, place_ref, pattern_ref, x_ref, weight_ref, *refs):
    segments = sum(len(job) for job in jobs)
    slopes, couplings = refs[:segments], refs[segments : 2 * segments]
    refs = refs[2 * segments :]
    added, outs = refs[:addends], refs[addends : addends + len(jobs)]
    rounded, warmth = refs[addends + len(jobs) :]
    step = pl.program_id(0)

    @pl.when(step == 0)
    def _():
        prior = x_ref[...]
        rounded[...] = prior.astype(jnp.bfloat16)
        total = jnp.sum(prior * weight_ref[...], axis=1, keepdims=True)
        warmth[...] = jnp.broadcast_to(total, warmth.shape)

    n = 0
    for index, job in enumerate(jobs):
        out_ref = outs[index]
        base = 0
        for segment in job:
            from_row, count = segment[:2]
            cells = pl.ds(from_row, count)
            rows = pl.ds(base, count)
            group = target(segment, place_ref[0], step)
            heat = warmth[cells, :]
            for t in range(SHELL):
                lanes = pl.ds(t * BLK, BLK)
                start = heat * slopes[n][0, :, lanes]
                if addends:
                    start += added[index][0, rows, lanes]
                out_ref[0, rows, lanes] = start
            for b in range(SHELL):
                product = jnp.dot(
                    rounded[cells, pl.ds(b * BLK, BLK)],
                    couplings[n][b, 0],
                    preferred_element_type=jnp.float32,
                )
                where = pattern_ref[b, group]
                lanes = pl.ds(pl.multiple_of(where * BLK, BLK), BLK)
                out_ref[0, rows, lanes] += product
            base += count
            n += 1


def partial_sums(jobs, units, addends, place, pattern, prior, weights, slope, coupling, room=28 << 20):
    segments = [segment for job in jobs for segment in job]
    slope_specs = [
        pl.BlockSpec(
            (1, 1, WIDTH), functools.partial(lambda n, i, m, p: (target(n, m[0], i), 0, 0), n)
        )
        for n in segments
    ]
    coupling_specs = [
        pl.BlockSpec(
            (SHELL, 1, BLK, BLK),
            functools.partial(lambda n, i, m, p: (0, target(n, m[0], i), 0, 0), n),
        )
        for n in segments
    ]
    heights = [sum(segment[1] for segment in job) for job in jobs]
    blocks = [pl.BlockSpec((1, rows, WIDTH), lambda i, g, p: (i, 0, 0)) for rows in heights]
    return pl.pallas_call(
        functools.partial(partial_kernel, jobs, len(addends)),
        grid_spec=pltpu.PrefetchScalarGridSpec(
            num_scalar_prefetch=2,
            grid=(units,),
            in_specs=[
                pl.BlockSpec((CELL, WIDTH), lambda i, g, p: (0, 0)),
                pl.BlockSpec((1, WIDTH), lambda i, g, p: (0, 0)),
            ]
            + slope_specs
            + coupling_specs
            + blocks[: len(addends)],
            out_specs=blocks,
            scratch_shapes=[
                pltpu.VMEM((CELL, WIDTH), jnp.bfloat16),
                pltpu.VMEM((CELL, BLK), jnp.float32),
            ],
        ),
        out_shape=[jax.ShapeDtypeStruct((units, rows, WIDTH), jnp.float32) for rows in heights],
        cost_estimate=pl.CostEstimate(
            flops=2 * sum(heights) * units * WIDTH * BLK,
            bytes_accessed=sum(heights) * units * WIDTH * 6,
            transcendentals=0,
        ),
        compiler_params=pltpu.CompilerParams(vmem_limit_bytes=room),
        name="partial_sums",
    )(
        place,
        pattern,
        prior,
        weights,
        *([slope] * len(segments)),
        *([coupling] * len(segments)),
        *addends,
    )


def powers_kernel(rate_ref, inscatter_ref, high_ref, low_ref):
    row = lax.broadcasted_iota(jnp.int32, (BLK, BLK), 0)
    column = lax.broadcasted_iota(jnp.int32, (BLK, BLK), 1)
    unit = jnp.where(row == column, 1.0, 0.0).astype(jnp.float32)

    def raise_power(k, now):
        raised = []
        for b in range(SHELL):
            high = now[b].astype(jnp.bfloat16)
            high_ref[b, k] = high
            low_ref[b, k] = (now[b] - high.astype(jnp.float32)).astype(jnp.bfloat16)
            raised.append(
                product(now[b] * rate_ref[:, pl.ds(b * BLK, BLK)], high_ref[b, 0], low_ref[b, 0])
            )
        return tuple(raised)

    lax.fori_loop(0, LAYERS, raise_power, tuple(unit + inscatter_ref[b] for b in range(SHELL)))


def product(face, high, low):
    top = face.astype(jnp.bfloat16)
    rest = (face - top.astype(jnp.float32)).astype(jnp.bfloat16)
    rows = face.shape[0]
    both = jnp.dot(
        jnp.concatenate([top, rest], axis=0), high, preferred_element_type=jnp.float32
    )
    return both[:rows] + both[rows:] + jnp.dot(top, low, preferred_element_type=jnp.float32)


def last_kernel(direction_ref, *refs):
    halves, wholes = refs[:8], refs[8:10]
    high_ref, low_ref, source_ref, out_ref = refs[10:]
    for side in range(2):
        rows = pl.ds(side * HALF, HALF)
        total = halves[4 * side][...]
        for part in halves[4 * side + 1 : 4 * side + 4]:
            total += part[...]
        for part in wholes:
            total += part[rows, :]
        source_ref[rows, :] = total
    for b in range(SHELL):
        lanes = pl.ds(b * BLK, BLK)
        up = direction_ref[b] == 1
        total = jnp.zeros((LATERAL, BLK), jnp.float32)
        for t in range(LAYERS):
            k = jnp.where(up, LAYERS - 1 - t, t)
            total += product(
                source_ref[pl.ds(t * LATERAL, LATERAL), lanes], high_ref[b, k], low_ref[b, k]
            )
        out_ref[:, lanes] = total


def particular_kernel(direction_ref, source_ref, rate_ref, high_ref, low_ref, out_ref):
    now = [jnp.zeros((LATERAL, BLK), jnp.float32) for _ in range(SHELL)]
    for t in range(LAYERS):
        for b in range(SHELL):
            lanes = pl.ds(b * BLK, BLK)
            at = jnp.where(direction_ref[b] == 1, t, LAYERS - 1 - t)
            rows = pl.ds(pl.multiple_of(at * LATERAL, LATERAL), LATERAL)
            now[b] = product(
                source_ref[rows, lanes] + rate_ref[:, lanes] * now[b], high_ref[b, 0], low_ref[b, 0]
            )
            out_ref[rows, lanes] = now[b]


def finish_kernel(
    direction_ref,
    slab_ref,
    wall_ref,
    one_ref,
    two_ref,
    three_ref,
    rate_ref,
    particular_ref,
    high_ref,
    low_ref,
    out_ref,
    faces,
):
    for k, face in enumerate((one_ref, two_ref, three_ref)):
        faces[k] = face[...]
    slab = slab_ref[0]
    now = [wall_ref[:, pl.ds(b * BLK, BLK)] for b in range(SHELL)]
    for n in range(3):
        for b in range(SHELL):
            lanes = pl.ds(b * BLK, BLK)
            up = direction_ref[b] == 1
            there = jnp.where(up, n, 3 - n)
            active = jnp.where(
                up, (there < slab).astype(jnp.int32), (there > slab).astype(jnp.int32)
            )
            k = jnp.maximum((there ^ slab) - 1, 0)
            moved = faces[k, :, lanes] + product(
                now[b] * rate_ref[:, lanes], high_ref[b, LAYERS - 1], low_ref[b, LAYERS - 1]
            )
            now[b] = jnp.where(active == 1, moved, now[b])
    for b in range(SHELL):
        lanes = pl.ds(b * BLK, BLK)
        up = direction_ref[b] == 1
        scaled = now[b] * rate_ref[:, lanes]
        for t in range(LAYERS):
            k = jnp.where(up, t, LAYERS - 1 - t)
            rows = pl.ds(t * LATERAL, LATERAL)
            out_ref[rows, lanes] = particular_ref[rows, lanes] + product(
                scaled, high_ref[b, k], low_ref[b, k]
            )


SMEM = pl.BlockSpec(memory_space=pltpu.SMEM)
VMEM = pl.BlockSpec(memory_space=pltpu.VMEM)


FIRST = pl.BlockSpec((SHELL, 1, BLK, BLK), lambda i: (0, 0, 0, 0))


def small_call(kernel, outs, specs, scratch=(), flops=0, grid=()):
    return pl.pallas_call(
        kernel,
        grid=grid,
        in_specs=specs,
        out_specs=[VMEM] * len(outs),
        out_shape=[jax.ShapeDtypeStruct(*out) for out in outs],
        scratch_shapes=list(scratch),
        cost_estimate=pl.CostEstimate(flops=flops, bytes_accessed=3 << 20, transcendentals=0),
        compiler_params=pltpu.CompilerParams(vmem_limit_bytes=16 << 20),
    )


def per_device(
    occupation_prior,
    coupling,
    pattern,
    pseudo_weights,
    equilibrium_slope,
    direction,
    stream_rate,
    inscatter,
    inflow_low,
    inflow_high,
    front_of_row,
):
    modes = lax.axis_index("modes").astype(jnp.int32)
    slab = lax.axis_index("slab").astype(jnp.int32)
    weights = pseudo_weights.reshape(1, WIDTH)
    rate = stream_rate.reshape(1, WIDTH)
    slope = equilibrium_slope.reshape(SIDE**3, 1, WIDTH)
    make = functools.partial(
        partial_sums,
        place=modes.reshape(1),
        pattern=pattern,
        weights=weights,
        slope=slope,
        coupling=coupling,
    )

    def ring_sums(low_step, high_step, prior, addends=(), **room):
        jobs = [
            (
                (0, CELL, 1 if upper else 3, upper, pair, step),
                (0 if upper else HALF, HALF, 2, upper, pair, step),
            )
            for upper in (True, False)
            for pair, step in ((0, low_step), (2, high_step))
        ]
        return make(tuple(jobs), 2, addends, prior=prior, **room)

    def ring(blocks, step):
        axes = (2, 2, 1, 1)
        signs = (step, -step, step, -step)
        moved = []
        for index, block in enumerate(blocks):
            moved.append(send(block, axes[index], signs[index]))
        return moved

    prior = occupation_prior
    split = [((SHELL, LAYERS, BLK, BLK), jnp.bfloat16)] * 2
    high, low = small_call(powers_kernel, split, [VMEM, VMEM], flops=200_000_000)(rate, inscatter)
    picks = front_of_row[:, None] == jnp.arange(inflow_low.shape[0], dtype=jnp.int32)[None, :]
    ahead = (jnp.repeat(direction, BLK) == 1)[None, :]
    inflow = jnp.where(ahead, inflow_low, inflow_high)
    wall = jnp.sum(jnp.where(picks[:, :, None], inflow[None, :, :], 0.0), axis=1)

    far_got = ring(ring_sums(2, 2, prior, room=62 << 20), 1)
    direct = ring_sums(3, 1, prior)
    early = ring(direct, -1)
    after, _ = lax.optimization_barrier((prior, direct))
    near = make(
        tuple(
            ((0 if upper else HALF, HALF, 0, upper, 0, step),)
            for upper in (True, False)
            for step in range(SIDE)
        ),
        SIDE,
        (),
        prior=after,
    )
    far_got, near = lax.optimization_barrier((far_got, near))
    beside = ((near[1], 2, 1), (near[3], 2, -1), (near[5], 1, 1), (near[7], 1, -1))
    late = ring(ring_sums(1, 3, prior, far_got), 1)
    early, high, low, wall = lax.optimization_barrier((early, high, low, wall))
    kept = ring_sums(0, 0, prior, early)
    a1, a3, a2 = kept[0][1] + late[0][1], kept[1][1] + late[1][1], kept[1][0] + late[1][0]
    b1, b3, b2 = kept[2][1] + late[2][1], kept[3][1] + late[3][1], kept[3][0] + late[3][0]
    near_got = []
    for block, axis, step in beside:
        near_got.append(send(block, axis, step))
    crossed = []
    for block, axis, step in ((a1, 1, 1), (a2, 1, 2), (a3, 1, -1), (b1, 2, 1), (b2, 2, 2), (b3, 2, -1)):
        crossed.append(send(block, axis, step))
    a_got, b_got = crossed[:3], crossed[3:]
    ready_a = near[0] + near_got[0] + near_got[1]
    ready_b = near[4] + near_got[2] + near_got[3]
    ready_a, ready_b = lax.optimization_barrier((ready_a, ready_b))
    across, _ = lax.optimization_barrier(((near[2], near[6]), (a_got, b_got)))
    far_x = send(across[0], 2, 2)
    far_y = send(across[1], 1, 2)
    a_own, a_got = lax.optimization_barrier(((kept[0], late[0]), a_got))
    b_own, b_got = lax.optimization_barrier(((kept[2], late[2]), b_got))
    a_sum = a_own[0][0] + a_own[1][0] + a_got[0] + a_got[1] + a_got[2]
    b_sum = b_own[0][0] + b_own[1][0] + b_got[0] + b_got[1] + b_got[2]
    far_up = send(a_sum[CELL:], 0, 1)
    far_down = send(b_sum[CELL:], 0, -1)
    above = jnp.concatenate([a_sum[:HALF] + far_up, a_sum[HALF:CELL]], axis=0)
    below = jnp.concatenate([b_sum[:HALF], b_sum[HALF:CELL] + far_down], axis=0)
    from_below = send(above, 0, 1)
    from_above = send(below, 0, -1)

    def ends(ready, got, axis):
        parts = [ready[i] + got[i] for i in range(SIDE)]
        moved = []
        for index, step in enumerate((1, 2, -1)):
            moved.append(send(parts[index + 1], axis, step))
        return [parts[0]] + moved

    halves = ends(ready_a, far_x, 1) + ends(ready_b, far_y, 2)

    whole = ((CELL, WIDTH), jnp.float32)
    source, last = small_call(
        last_kernel,
        [whole, ((LATERAL, WIDTH), jnp.float32)],
        [SMEM] + [VMEM] * 12,
        flops=40_000_000,
    )(direction, *halves, from_below, from_above, high, low)
    faces = [
        lax.ppermute(last, "slab", [(i, i ^ k) for i in range(4)]) for k in (1, 2, 3)
    ]
    (particular,) = small_call(
        particular_kernel, [whole], [SMEM, VMEM, VMEM, FIRST, FIRST], flops=40_000_000, grid=(1,)
    )(direction, source, rate, high, low)
    (swept,) = small_call(
        finish_kernel,
        [whole],
        [SMEM, SMEM] + [VMEM] * 8,
        scratch=[pltpu.VMEM((3, LATERAL, WIDTH), jnp.float32)],
        flops=60_000_000,
    )(direction, slab.reshape(1), wall, *faces, rate, particular, high, low)
    return swept


def solution(mesh):
    placed = (
        P("slab", "modes"),
        P("modes", None, None, None),
        P("modes", None),
        P("modes"),
        P(),
        P("modes"),
        P("modes"),
        P("modes", None, None),
        P(None, "modes"),
        P(None, "modes"),
        P(),
    )

    return jax.shard_map(
        per_device, mesh=mesh, in_specs=placed, out_specs=P("slab", "modes"), check_vma=False
    )
```

```python
import functools

import jax
import jax.numpy as jnp
from jax import lax
from jax.experimental import pallas as pl
from jax.experimental.pallas import tpu as pltpu
from jax.sharding import PartitionSpec as P


BLK = 128
SHELL = 4
SIDE = 4
LAYERS = 8
LATERAL = 16
WIDTH = SHELL * BLK
CELL = LAYERS * LATERAL
HALF = CELL // 2


def route(axis, step):
    pairs = []
    for z in range(SIDE):
        for y in range(SIDE):
            for x in range(SIDE):
                there = [z, y, x]
                there[axis] = (there[axis] + step) % SIDE
                pairs.append(
                    ((z * SIDE + y) * SIDE + x, (there[0] * SIDE + there[1]) * SIDE + there[2])
                )
    return pairs


def send(block, axis, step):
    return lax.ppermute(block, "modes", route(axis, step))


def target(segment, place, i):
    _, _, z_step, upper, pair, step = segment
    along = pair + i
    y, x = (along, step) if upper else (step, along)
    z = ((place >> 4) + z_step) & 3
    return z * 16 + (((place >> 2) + y) & 3) * 4 + ((place + x) & 3)


def partial_kernel(jobs, addends, place_ref, pattern_ref, x_ref, weight_ref, *refs):
    segments = sum(len(job) for job in jobs)
    slopes, couplings = refs[:segments], refs[segments : 2 * segments]
    refs = refs[2 * segments :]
    added, outs = refs[:addends], refs[addends : addends + len(jobs)]
    rounded, warmth = refs[addends + len(jobs) :]
    step = pl.program_id(0)

    @pl.when(step == 0)
    def _():
        prior = x_ref[...]
        rounded[...] = prior.astype(jnp.bfloat16)
        total = jnp.sum(prior * weight_ref[...], axis=1, keepdims=True)
        warmth[...] = jnp.broadcast_to(total, warmth.shape)

    n = 0
    for index, job in enumerate(jobs):
        out_ref = outs[index]
        base = 0
        for segment in job:
            from_row, count = segment[:2]
            cells = pl.ds(from_row, count)
            rows = pl.ds(base, count)
            group = target(segment, place_ref[0], step)
            heat = warmth[cells, :]
            for t in range(SHELL):
                lanes = pl.ds(t * BLK, BLK)
                start = heat * slopes[n][0, :, lanes]
                if addends:
                    start += added[index][0, rows, lanes]
                out_ref[0, rows, lanes] = start
            for b in range(SHELL):
                product = jnp.dot(
                    rounded[cells, pl.ds(b * BLK, BLK)],
                    couplings[n][b, 0],
                    preferred_element_type=jnp.float32,
                )
                where = pattern_ref[b, group]
                lanes = pl.ds(pl.multiple_of(where * BLK, BLK), BLK)
                out_ref[0, rows, lanes] += product
            base += count
            n += 1


def partial_sums(jobs, units, addends, place, pattern, prior, weights, slope, coupling, room=28 << 20):
    segments = [segment for job in jobs for segment in job]
    slope_specs = [
        pl.BlockSpec(
            (1, 1, WIDTH), functools.partial(lambda n, i, m, p: (target(n, m[0], i), 0, 0), n)
        )
        for n in segments
    ]
    coupling_specs = [
        pl.BlockSpec(
            (SHELL, 1, BLK, BLK),
            functools.partial(lambda n, i, m, p: (0, target(n, m[0], i), 0, 0), n),
        )
        for n in segments
    ]
    heights = [sum(segment[1] for segment in job) for job in jobs]
    blocks = [pl.BlockSpec((1, rows, WIDTH), lambda i, g, p: (i, 0, 0)) for rows in heights]
    return pl.pallas_call(
        functools.partial(partial_kernel, jobs, len(addends)),
        grid_spec=pltpu.PrefetchScalarGridSpec(
            num_scalar_prefetch=2,
            grid=(units,),
            in_specs=[
                pl.BlockSpec((CELL, WIDTH), lambda i, g, p: (0, 0)),
                pl.BlockSpec((1, WIDTH), lambda i, g, p: (0, 0)),
            ]
            + slope_specs
            + coupling_specs
            + blocks[: len(addends)],
            out_specs=blocks,
            scratch_shapes=[
                pltpu.VMEM((CELL, WIDTH), jnp.bfloat16),
                pltpu.VMEM((CELL, BLK), jnp.float32),
            ],
        ),
        out_shape=[jax.ShapeDtypeStruct((units, rows, WIDTH), jnp.float32) for rows in heights],
        cost_estimate=pl.CostEstimate(
            flops=2 * sum(heights) * units * WIDTH * BLK,
            bytes_accessed=sum(heights) * units * WIDTH * 6,
            transcendentals=0,
        ),
        compiler_params=pltpu.CompilerParams(vmem_limit_bytes=room),
        name="partial_sums",
    )(
        place,
        pattern,
        prior,
        weights,
        *([slope] * len(segments)),
        *([coupling] * len(segments)),
        *addends,
    )


def powers_kernel(rate_ref, inscatter_ref, high_ref, low_ref):
    row = lax.broadcasted_iota(jnp.int32, (BLK, BLK), 0)
    column = lax.broadcasted_iota(jnp.int32, (BLK, BLK), 1)
    unit = jnp.where(row == column, 1.0, 0.0).astype(jnp.float32)

    def raise_power(k, now):
        raised = []
        for b in range(SHELL):
            high = now[b].astype(jnp.bfloat16)
            high_ref[b, k] = high
            low_ref[b, k] = (now[b] - high.astype(jnp.float32)).astype(jnp.bfloat16)
            raised.append(
                product(now[b] * rate_ref[:, pl.ds(b * BLK, BLK)], high_ref[b, 0], low_ref[b, 0])
            )
        return tuple(raised)

    lax.fori_loop(0, LAYERS, raise_power, tuple(unit + inscatter_ref[b] for b in range(SHELL)))


def product(face, high, low):
    top = face.astype(jnp.bfloat16)
    rest = (face - top.astype(jnp.float32)).astype(jnp.bfloat16)
    rows = face.shape[0]
    both = jnp.dot(
        jnp.concatenate([top, rest], axis=0), high, preferred_element_type=jnp.float32
    )
    return both[:rows] + both[rows:] + jnp.dot(top, low, preferred_element_type=jnp.float32)


def last_kernel(direction_ref, *refs):
    halves, wholes = refs[:8], refs[8:10]
    high_ref, low_ref, source_ref, out_ref = refs[10:]
    for side in range(2):
        rows = pl.ds(side * HALF, HALF)
        total = halves[4 * side][...]
        for part in halves[4 * side + 1 : 4 * side + 4]:
            total += part[...]
        for part in wholes:
            total += part[rows, :]
        source_ref[rows, :] = total
    for b in range(SHELL):
        lanes = pl.ds(b * BLK, BLK)
        up = direction_ref[b] == 1
        total = jnp.zeros((LATERAL, BLK), jnp.float32)
        for t in range(LAYERS):
            k = jnp.where(up, LAYERS - 1 - t, t)
            total += product(
                source_ref[pl.ds(t * LATERAL, LATERAL), lanes], high_ref[b, k], low_ref[b, k]
            )
        out_ref[:, lanes] = total


def particular_kernel(direction_ref, source_ref, rate_ref, high_ref, low_ref, out_ref):
    def layer(t, now):
        following = []
        for b in range(SHELL):
            lanes = pl.ds(b * BLK, BLK)
            at = jnp.where(direction_ref[b] == 1, t, LAYERS - 1 - t)
            rows = pl.ds(pl.multiple_of(at * LATERAL, LATERAL), LATERAL)
            face = product(
                source_ref[rows, lanes] + rate_ref[:, lanes] * now[b], high_ref[b, 0], low_ref[b, 0]
            )
            out_ref[rows, lanes] = face
            following.append(face)
        return tuple(following)

    lax.fori_loop(0, LAYERS, layer, (jnp.zeros((LATERAL, BLK), jnp.float32),) * SHELL)


def finish_kernel(
    direction_ref,
    slab_ref,
    wall_ref,
    one_ref,
    two_ref,
    three_ref,
    rate_ref,
    particular_ref,
    high_ref,
    low_ref,
    out_ref,
    faces,
):
    for k, face in enumerate((one_ref, two_ref, three_ref)):
        faces[k] = face[...]
    slab = slab_ref[0]
    now = [wall_ref[:, pl.ds(b * BLK, BLK)] for b in range(SHELL)]
    for n in range(3):
        for b in range(SHELL):
            lanes = pl.ds(b * BLK, BLK)
            up = direction_ref[b] == 1
            there = jnp.where(up, n, 3 - n)
            active = jnp.where(
                up, (there < slab).astype(jnp.int32), (there > slab).astype(jnp.int32)
            )
            k = jnp.maximum((there ^ slab) - 1, 0)
            moved = faces[k, :, lanes] + product(
                now[b] * rate_ref[:, lanes], high_ref[b, LAYERS - 1], low_ref[b, LAYERS - 1]
            )
            now[b] = jnp.where(active == 1, moved, now[b])
    for b in range(SHELL):
        lanes = pl.ds(b * BLK, BLK)
        up = direction_ref[b] == 1
        scaled = now[b] * rate_ref[:, lanes]
        for t in range(LAYERS):
            k = jnp.where(up, t, LAYERS - 1 - t)
            rows = pl.ds(t * LATERAL, LATERAL)
            out_ref[rows, lanes] = particular_ref[rows, lanes] + product(
                scaled, high_ref[b, k], low_ref[b, k]
            )


SMEM = pl.BlockSpec(memory_space=pltpu.SMEM)
VMEM = pl.BlockSpec(memory_space=pltpu.VMEM)


FIRST = pl.BlockSpec((SHELL, 1, BLK, BLK), lambda i: (0, 0, 0, 0))


def small_call(kernel, outs, specs, scratch=(), flops=0, grid=()):
    return pl.pallas_call(
        kernel,
        grid=grid,
        in_specs=specs,
        out_specs=[VMEM] * len(outs),
        out_shape=[jax.ShapeDtypeStruct(*out) for out in outs],
        scratch_shapes=list(scratch),
        cost_estimate=pl.CostEstimate(flops=flops, bytes_accessed=3 << 20, transcendentals=0),
        compiler_params=pltpu.CompilerParams(vmem_limit_bytes=16 << 20),
    )


def per_device(
    occupation_prior,
    coupling,
    pattern,
    pseudo_weights,
    equilibrium_slope,
    direction,
    stream_rate,
    inscatter,
    inflow_low,
    inflow_high,
    front_of_row,
):
    modes = lax.axis_index("modes").astype(jnp.int32)
    slab = lax.axis_index("slab").astype(jnp.int32)
    weights = pseudo_weights.reshape(1, WIDTH)
    rate = stream_rate.reshape(1, WIDTH)
    slope = equilibrium_slope.reshape(SIDE**3, 1, WIDTH)
    make = functools.partial(
        partial_sums,
        place=modes.reshape(1),
        pattern=pattern,
        weights=weights,
        slope=slope,
        coupling=coupling,
    )

    def ring_sums(low_step, high_step, prior, addends=(), **room):
        jobs = [
            (
                (0, CELL, 1 if upper else 3, upper, pair, step),
                (0 if upper else HALF, HALF, 2, upper, pair, step),
            )
            for upper in (True, False)
            for pair, step in ((0, low_step), (2, high_step))
        ]
        return make(tuple(jobs), 2, addends, prior=prior, **room)

    def ring(blocks, step):
        axes = (2, 2, 1, 1)
        signs = (step, -step, step, -step)
        moved = []
        for index, block in enumerate(blocks):
            moved.append(send(block, axes[index], signs[index]))
        return moved

    prior = occupation_prior
    split = [((SHELL, LAYERS, BLK, BLK), jnp.bfloat16)] * 2
    high, low = small_call(powers_kernel, split, [VMEM, VMEM], flops=200_000_000)(rate, inscatter)
    picks = front_of_row[:, None] == jnp.arange(inflow_low.shape[0], dtype=jnp.int32)[None, :]
    ahead = (jnp.repeat(direction, BLK) == 1)[None, :]
    inflow = jnp.where(ahead, inflow_low, inflow_high)
    wall = jnp.sum(jnp.where(picks[:, :, None], inflow[None, :, :], 0.0), axis=1)

    far_got = ring(ring_sums(2, 2, prior, room=62 << 20), 1)
    direct = ring_sums(3, 1, prior)
    early = ring(direct, -1)
    after, _ = lax.optimization_barrier((prior, direct))
    near = make(
        tuple(
            ((0 if upper else HALF, HALF, 0, upper, 0, step),)
            for upper in (True, False)
            for step in range(SIDE)
        ),
        SIDE,
        (),
        prior=after,
    )
    far_got, near = lax.optimization_barrier((far_got, near))
    beside = (
        (near[2][:2], 2, 1),
        (near[2][2:], 2, -1),
        (near[6][:2], 1, 1),
        (near[6][2:], 1, -1),
    )
    late = ring(ring_sums(1, 3, prior, far_got), 1)
    early, high, low, wall = lax.optimization_barrier((early, high, low, wall))
    kept = ring_sums(0, 0, prior, early)
    a1, a3, a2 = kept[0][1] + late[0][1], kept[1][1] + late[1][1], kept[1][0] + late[1][0]
    b1, b3, b2 = kept[2][1] + late[2][1], kept[3][1] + late[3][1], kept[3][0] + late[3][0]
    near_got = []
    for block, axis, step in beside:
        near_got.append(send(block, axis, step))
    crossed = []
    for block, axis, step in ((a1, 1, 1), (a2, 1, 2), (a3, 1, -1), (b1, 2, 1), (b2, 2, 2), (b3, 2, -1)):
        crossed.append(send(block, axis, step))
    a_got, b_got = crossed[:3], crossed[3:]
    near_got, _ = lax.optimization_barrier((near_got, (a1, a2, a3, b1, b2, b3)))
    onward = (
        jnp.concatenate([near[1][:2] + near_got[0], near[1][2:]], axis=0),
        jnp.concatenate([near[3][:2], near[3][2:] + near_got[1]], axis=0),
        jnp.concatenate([near[5][:2] + near_got[2], near[5][2:]], axis=0),
        jnp.concatenate([near[7][:2], near[7][2:] + near_got[3]], axis=0),
    )
    onward, _ = lax.optimization_barrier((onward, (a_got, b_got)))
    arrived = []
    for index, (axis, step) in enumerate(((2, 1), (2, -1), (1, 1), (1, -1))):
        arrived.append(send(onward[index], axis, step))
    a_own, a_got = lax.optimization_barrier(((kept[0], late[0]), a_got))
    b_own, b_got = lax.optimization_barrier(((kept[2], late[2]), b_got))
    a_sum = a_own[0][0] + a_own[1][0] + a_got[0] + a_got[1] + a_got[2]
    b_sum = b_own[0][0] + b_own[1][0] + b_got[0] + b_got[1] + b_got[2]
    far_up = send(a_sum[CELL:], 0, 1)
    far_down = send(b_sum[CELL:], 0, -1)
    above = jnp.concatenate([a_sum[:HALF] + far_up, a_sum[HALF:CELL]], axis=0)
    below = jnp.concatenate([b_sum[:HALF], b_sum[HALF:CELL] + far_down], axis=0)
    from_below = send(above, 0, 1)
    from_above = send(below, 0, -1)

    def ends(own, below_got, above_got, axis):
        parts = [own[i] + below_got[i] + above_got[i] for i in range(SIDE)]
        moved = []
        for index, step in enumerate((1, 2, -1)):
            moved.append(send(parts[index + 1], axis, step))
        return [parts[0]] + moved

    halves = ends(near[0], arrived[0], arrived[1], 1) + ends(near[4], arrived[2], arrived[3], 2)

    whole = ((CELL, WIDTH), jnp.float32)
    source, last = small_call(
        last_kernel,
        [whole, ((LATERAL, WIDTH), jnp.float32)],
        [SMEM] + [VMEM] * 12,
        flops=40_000_000,
    )(direction, *halves, from_below, from_above, high, low)
    faces = [
        lax.ppermute(last, "slab", [(i, i ^ k) for i in range(4)]) for k in (1, 2, 3)
    ]
    (particular,) = small_call(
        particular_kernel, [whole], [SMEM, VMEM, VMEM, FIRST, FIRST], flops=40_000_000, grid=(1,)
    )(direction, source, rate, high, low)
    (swept,) = small_call(
        finish_kernel,
        [whole],
        [SMEM, SMEM] + [VMEM] * 8,
        scratch=[pltpu.VMEM((3, LATERAL, WIDTH), jnp.float32)],
        flops=60_000_000,
    )(direction, slab.reshape(1), wall, *faces, rate, particular, high, low)
    return swept


def solution(mesh):
    placed = (
        P("slab", "modes"),
        P("modes", None, None, None),
        P("modes", None),
        P("modes"),
        P(),
        P("modes"),
        P("modes"),
        P("modes", None, None),
        P(None, "modes"),
        P(None, "modes"),
        P(),
    )

    return jax.shard_map(
        per_device, mesh=mesh, in_specs=placed, out_specs=P("slab", "modes"), check_vma=False
    )
```
